32 devices in a mesh: dp: 4 (over y, core), label: 8 (over z, x).
Axes of the slice: x: 2, y: 2, z: 4, core: 2. Of those that a mesh axis runs over, the one named last changes fastest.
Arguments:
- calib: bfloat16 [16384, 2688], P(('dp', 'label')), may hold values from -160 to 160
- block_weight: bfloat16 [8192, 128], P('dp', 'label'), may hold values from -0.125 to 0.125
- rest_weight: bfloat16 [8192, 2560], P('dp', 'label'), may hold values from -0.125 to 0.125
- prune_mask: int32 [8192, 128], P(('dp', 'label')), may hold values 0 or 1
Outputs:
- pruned_block: bfloat16 [8192, 128], P(('dp', 'label'))
- updated_rest: bfloat16 [8192, 2560], P('dp', 'label')
The draws below stay inside these ranges and needn't reach their ends.
All inputs are finite; a program needn't handle non-finite values. No bound on the sum of `prune_mask` on one device may be relied on, other than what follows from the above.
Results may differ from the reference program's by a relative error of at most 0.00075.
Values may be sent and summed in bfloat16 or wider, within the bound.
A program may use at most 64 MiB of HBM per device.

```python
import math
import jax
import jax.numpy as jnp
from jax import lax

DH = 2688
BLOCK = 128
ITERS = 6
NCAL = 16384
VOCAB = 8192


def draw_calib(key, part):
    key_scale = jax.random.fold_in(key, 11)
    key_base = jax.random.fold_in(key, 12)
    column_scale = jnp.exp(jax.random.uniform(key_scale, (DH,), jnp.float32, 0.0, math.log(10.0)))
    position = jnp.arange(NCAL, dtype=jnp.float32)[:, None] / (NCAL - 1)
    ramp = jnp.exp(math.log(2.5) * position)
    noise = jnp.clip(jax.random.normal(key_base, (NCAL, DH), jnp.float32), -6.0, 6.0)
    mixed = noise + 0.3 * jnp.roll(noise, 1, axis=1) + 0.15 * jnp.roll(noise, 7, axis=1)
    return (mixed * ramp * column_scale[None, :] * 0.6).astype(jnp.bfloat16)


def set_ends(entries, own_key, low, top_value):
    longest = entries.shape.index(max(entries.shape))
    spots = []
    for shift in (0, 1):
        where = [jax.random.randint(jax.random.fold_in(own_key, axis), (), 0, length) for axis, length in enumerate(entries.shape)]
        where[longest] = (where[longest] + shift) % entries.shape[longest]
        spots.append(tuple(where))
    return entries.at[spots[0]].set(low).at[spots[1]].set(top_value)


def level_of(stream_key, shape, shards, smallest, top_value):
    loudness = 1.0
    for dim, parts in shards:
        steps = jax.random.uniform(jax.random.fold_in(jax.random.fold_in(stream_key, 6), dim), (parts,), jnp.float32, smallest / len(shards), top_value / len(shards))
        loudness = loudness * jnp.repeat(jnp.exp(steps), shape[dim] // parts).reshape((-1,) + (1,) * (len(shape) - 1 - dim))
    return loudness


def normal_values(own_key, shape, scale, bound, split=(), held_as=jnp.bfloat16):
    values = scale * jax.random.normal(own_key, shape, jnp.float32)
    if split:
        values = values * level_of(own_key, shape, split, -0.22, 0.18)
    return jnp.clip(values, -bound, bound).astype(held_as)


def setup_inputs(seed: int = 0) -> dict:
    streams_of = jax.random.split(jax.random.key(seed), 5)
    return {
        "calib": draw_calib(jax.random.fold_in(streams_of[4], 71), 0),
        "block_weight": normal_values(streams_of[1], (VOCAB, BLOCK), DH ** -0.5, 0.125, ((0, 4), (1, 8))),
        "rest_weight": normal_values(streams_of[2], (VOCAB, DH - BLOCK), DH ** -0.5, 0.125, ((0, 4), (1, 8))),
        "prune_mask": set_ends((jax.random.randint(streams_of[3], (VOCAB, BLOCK), 0, 2) < 1).astype(jnp.int32), jax.random.fold_in(streams_of[3], 1), 0, 1),
    }


damp_fraction = 0.01

def prune_rows(weights, mask, upper):
    maskf = mask.astype(jnp.float32)
    width = weights.shape[1]

    def advance(index, carry):
        current, kept, errors = carry
        column = lax.dynamic_slice_in_dim(current, index, 1, 1)[:, 0]
        chosen = lax.dynamic_slice_in_dim(maskf, index, 1, 1)[:, 0]
        pivot = lax.dynamic_slice_in_dim(upper, index, 1, 0)[0]
        diagonal = lax.dynamic_index_in_dim(pivot, index, keepdims=False)
        error = chosen * column / diagonal
        kept = lax.dynamic_update_slice_in_dim(kept, ((1.0 - chosen) * column)[:, None], index, 1)
        errors = lax.dynamic_update_slice_in_dim(errors, error[:, None], index, 1)
        current = current - error[:, None] * pivot[None, :]
        return (current, kept, errors)
    start = (weights.astype(jnp.float32), jnp.zeros(weights.shape, jnp.float32), jnp.zeros(weights.shape, jnp.float32))
    result = lax.fori_loop(0, width, advance, start)
    return (result[1], result[2])

def reference(calib, block_weight, rest_weight, prune_mask):
    total = calib.shape[0]
    width = calib.shape[1]
    block = block_weight.shape[1]
    colsq = jnp.sum(jnp.square(calib.astype(jnp.float32)), axis=0)
    damping = damp_fraction * 2.0 * jnp.sum(colsq) / (total * width)
    scale = 2.0 / total
    hdiag = (scale * colsq + damping)[:, None]
    resid = jnp.eye(width, block, dtype=jnp.float32)
    precond = resid / hdiag
    direction = precond
    solution = jnp.zeros((width, block), jnp.float32)
    rho = jnp.sum(resid * precond, axis=0)
    for step in range(ITERS):
        inner = jnp.einsum('tk,kb->tb', calib.astype(jnp.float32), direction.astype(jnp.float32), precision=lax.Precision.HIGHEST, preferred_element_type=jnp.float32)
        outer = jnp.einsum('tk,tb->kb', calib.astype(jnp.float32), inner.astype(jnp.float32), precision=lax.Precision.HIGHEST, preferred_element_type=jnp.float32)
        image = scale * outer + damping * direction
        alpha = rho / jnp.sum(direction * image, axis=0)
        solution = solution + alpha * direction
        resid = resid - alpha * image
        precond = resid / hdiag
        fresh = jnp.sum(resid * precond, axis=0)
        direction = precond + fresh / rho * direction
        rho = fresh
    top = 0.5 * (solution[:block] + solution[:block].T)
    lower = jnp.linalg.cholesky(top)
    upper = lower.T
    cross = jax.scipy.linalg.solve_triangular(lower, solution[block:].T, lower=True)
    kept, errors = prune_rows(block_weight, prune_mask, upper)
    delta = jnp.dot(errors.astype(jnp.float32), cross.astype(jnp.float32), precision=lax.Precision.HIGHEST, preferred_element_type=jnp.float32)
    updated = (rest_weight.astype(jnp.float32) - delta).astype(jnp.bfloat16)
    return (kept.astype(jnp.bfloat16), updated)
```

```python
import functools

import jax
import jax.numpy as jnp
from jax import lax
from jax.experimental import pallas as pl
from jax.experimental.pallas import tpu as pltpu
from jax.sharding import PartitionSpec as P

ITERS = 6
MESH = pl.DeviceIdType.MESH

damp_fraction = 0.01
sub_width = 16


def reduce_kernel(nd, nl, x_ref, o_ref, pbuf, sbuf, rbuf, psend, precv, ssend, srecv, gsend, grecv, fsend, frecv):
    dp = lax.axis_index("dp")
    label = lax.axis_index("label")
    core = lax.rem(dp, 2)
    chip = (dp // 2) * nl + label
    n = (nd // 2) * nl
    partner = (dp + 1 - 2 * core, label)

    def ahead(d):
        return lax.rem(chip + d, n)

    def behind(d):
        return lax.rem(chip + n - d, n)

    def device(j):
        return (2 * (j // nl) + core, lax.rem(j, nl))

    def remote(src, dst, send, recv, to):
        return pltpu.make_async_remote_copy(
            src_ref=src, dst_ref=dst, send_sem=send, recv_sem=recv, device_id=to, device_id_type=MESH
        )

    def pair(d):
        return remote(x_ref.at[1 - core, ahead(d)], pbuf.at[d], psend.at[d], precv.at[d], partner)

    def scatter(d):
        return remote(sbuf.at[d], rbuf.at[d], ssend.at[d], srecv.at[d], device(ahead(d)))

    def gather(d):
        return remote(o_ref.at[core, chip], o_ref.at[core, chip], gsend.at[d], grecv.at[d], device(ahead(d)))

    def gathered(d):
        return remote(o_ref.at[core, behind(d)], o_ref.at[core, behind(d)], gsend.at[d], grecv.at[d], device(behind(d)))

    def forward(d):
        return remote(o_ref.at[core, behind(d)], o_ref.at[core, behind(d)], fsend.at[d], frecv.at[d], partner)

    def forwarded(d):
        return remote(
            o_ref.at[1 - core, behind(d)], o_ref.at[1 - core, behind(d)], fsend.at[d], frecv.at[d], partner
        )

    def each(low, body):
        def step(d, carry):
            body(d)
            return carry

        lax.fori_loop(low, n, step, 0)

    barrier = pltpu.get_barrier_semaphore()
    pl.semaphore_signal(barrier, inc=1, device_id=partner, device_id_type=MESH)
    each(1, lambda d: pl.semaphore_signal(barrier, inc=1, device_id=device(ahead(d)), device_id_type=MESH))
    pl.semaphore_wait(barrier, n)

    each(1, lambda d: pair(d).start())
    pair(0).start()

    def send_sum(d):
        pair(d).wait_recv()
        sbuf[d] = x_ref[core, ahead(d)] + pbuf[d]
        scatter(d).start()

    each(1, send_sum)
    pair(0).wait_recv()

    def add(d, acc):
        scatter(d).wait_recv()
        return acc + rbuf[d]

    o_ref[core, chip] = lax.fori_loop(1, n, add, x_ref[core, chip] + pbuf[0])
    each(1, lambda d: gather(d).start())
    forward(0).start()

    def pass_on(d):
        gathered(d).wait_recv()
        forward(d).start()

    each(1, pass_on)
    each(0, lambda d: forwarded(d).wait_recv())
    each(0, lambda d: pair(d).wait_send())
    each(1, lambda d: scatter(d).wait_send())
    each(1, lambda d: gather(d).wait_send())
    each(0, lambda d: forward(d).wait_send())


def piece_rows(rows, nd, nl):
    return -(-rows // (nd * nl * 8)) * 8


def all_sum(x, nd, nl):
    n = nd // 2 * nl
    piece = x.shape[0] // (2 * n)
    lanes = x.shape[1]
    shape = (2, n, piece, lanes)
    sems = pltpu.SemaphoreType.DMA((n,))
    out = pl.pallas_call(
        functools.partial(reduce_kernel, nd, nl),
        out_shape=jax.ShapeDtypeStruct(shape, jnp.float32),
        in_specs=[pl.BlockSpec(memory_space=pltpu.VMEM)],
        out_specs=pl.BlockSpec(memory_space=pltpu.VMEM),
        scratch_shapes=[pltpu.VMEM((n, piece, lanes), jnp.float32)] * 3 + [sems] * 8,
        compiler_params=pltpu.CompilerParams(
            collective_id=0, has_side_effects=True, vmem_limit_bytes=24 << 20
        ),
        name="all_sum",
    )(x.reshape(shape))
    return out.reshape(x.shape)


def small_kernel(nd, nl, x_ref, o_ref, buf, send, recv):
    n = nd * nl
    me = lax.axis_index("dp") * nl + lax.axis_index("label")

    def device(j):
        return (j // nl, lax.rem(j, nl))

    def out(d):
        return pltpu.make_async_remote_copy(
            src_ref=x_ref,
            dst_ref=buf.at[me],
            send_sem=send.at[d],
            recv_sem=recv.at[d],
            device_id=device(lax.rem(me + d, n)),
            device_id_type=MESH,
        )

    def arrived(d):
        j = lax.rem(me + n - d, n)
        return pltpu.make_async_remote_copy(
            src_ref=x_ref,
            dst_ref=buf.at[j],
            send_sem=send.at[d],
            recv_sem=recv.at[d],
            device_id=device(j),
            device_id_type=MESH,
        )

    def each(body):
        def step(d, carry):
            body(d)
            return carry

        lax.fori_loop(1, n, step, 0)

    barrier = pltpu.get_barrier_semaphore()
    each(lambda d: pl.semaphore_signal(barrier, inc=1, device_id=device(lax.rem(me + d, n)), device_id_type=MESH))
    pl.semaphore_wait(barrier, n - 1)
    each(lambda d: out(d).start())
    buf[me] = x_ref[...]
    each(lambda d: arrived(d).wait_recv())
    o_ref[...] = lax.fori_loop(1, n, lambda j, acc: acc + buf[j], buf[0])
    each(lambda d: out(d).wait_send())


def small_sum(x, nd, nl):
    n = nd * nl
    return pl.pallas_call(
        functools.partial(small_kernel, nd, nl),
        out_shape=jax.ShapeDtypeStruct(x.shape, jnp.float32),
        in_specs=[pl.BlockSpec(memory_space=pltpu.VMEM)],
        out_specs=pl.BlockSpec(memory_space=pltpu.VMEM),
        scratch_shapes=[
            pltpu.VMEM((n,) + x.shape, jnp.float32),
            pltpu.SemaphoreType.DMA((n,)),
            pltpu.SemaphoreType.DMA((n,)),
        ],
        compiler_params=pltpu.CompilerParams(collective_id=1, has_side_effects=True),
        name="small_sum",
    )(x)


def prune_kernel(w_ref, m_ref, l_ref, kept_ref, err_ref):
    block = w_ref.shape[0]
    err_ref[...] = jnp.zeros_like(err_ref)
    for begin in range(0, block, sub_width):
        rows = pl.ds(begin, sub_width)
        window = w_ref[rows, :].astype(jnp.float32)
        chosen = m_ref[rows, :].astype(jnp.float32)
        factor = l_ref[rows, :]
        if begin:
            window = window - jnp.dot(
                factor, err_ref[...], precision=lax.Precision.HIGHEST, preferred_element_type=jnp.float32
            )
        for offset in range(sub_width):
            index = begin + offset
            column = factor[:, index : index + 1]
            inverse = 1.0 / factor[offset : offset + 1, index : index + 1]
            error = chosen[offset : offset + 1, :] * window[offset : offset + 1, :] * inverse
            err_ref[index : index + 1, :] = error
            window = window - column * error
        kept_ref[rows, :] = ((1.0 - chosen) * window).astype(kept_ref.dtype)


def prune_rows(weights, mask, lower):
    block, rows = weights.shape
    tile = min(rows, 2048)
    spec = pl.BlockSpec((block, tile), lambda i: (0, i))
    return pl.pallas_call(
        prune_kernel,
        grid=(rows // tile,),
        out_shape=(
            jax.ShapeDtypeStruct((block, rows), jnp.bfloat16),
            jax.ShapeDtypeStruct((block, rows), jnp.float32),
        ),
        in_specs=[spec, spec, pl.BlockSpec((block, block), lambda i: (0, 0))],
        out_specs=(spec, spec),
        compiler_params=pltpu.CompilerParams(vmem_limit_bytes=32 << 20),
        name="prune_rows",
    )(weights, mask, lower)


def per_device(calib, block_weight, rest_weight, prune_mask):
    tokens = calib.shape[0]
    width = calib.shape[1]
    block = prune_mask.shape[1]
    nd, nl = lax.axis_size("dp"), lax.axis_size("label")
    total = tokens * nd * nl
    weights = lax.all_gather(block_weight.T, "label", axis=0, tiled=True)
    mask = lax.all_gather(prune_mask.T.astype(jnp.bfloat16), "label", axis=1, tiled=True)

    stat_rows = width // block
    padded = piece_rows(width + stat_rows, nd, nl) * nd * nl
    local_sq = jnp.sum(jnp.square(calib.astype(jnp.float32)), axis=0)
    first = lax.dot_general(
        calib, calib[:, :block], (((0,), (0,)), ((), ())), preferred_element_type=jnp.float32
    )
    summed = all_sum(
        jnp.concatenate(
            [first, local_sq.reshape(stat_rows, block), jnp.zeros((padded - width - stat_rows, block), jnp.float32)]
        ),
        nd,
        nl,
    )
    colsq = summed[width : width + stat_rows].reshape(width)
    damping = damp_fraction * 2.0 * jnp.sum(colsq) / (total * width)
    scale = 2.0 / total
    hdiag = scale * colsq + damping
    diag_rows = hdiag[:, None]
    resid = jnp.eye(width, block, dtype=jnp.float32)
    precond = resid / diag_rows
    direction = precond
    solution = jnp.zeros((width, block), jnp.float32)
    rho = jnp.sum(resid * precond, axis=0)
    for step in range(ITERS):
        if step:
            inner = jnp.einsum(
                "tk,kb->tb",
                calib,
                direction,
                precision=lax.Precision.HIGHEST,
                preferred_element_type=jnp.float32,
            )
        if step == ITERS - 1:
            local = jnp.sum(inner * inner, axis=0)
            local = jnp.pad(local[None, :], ((0, 7), (0, 0)))
            energy = scale * small_sum(local, nd, nl)[0] + damping * jnp.sum(direction * direction, axis=0)
            solution = solution + rho / energy * direction
            break
        if step:
            outer = jnp.einsum(
                "tk,tb->kb",
                calib,
                inner,
                precision=lax.Precision.HIGHEST,
                preferred_element_type=jnp.float32,
            )
            outer = all_sum(jnp.pad(outer, ((0, padded - width), (0, 0))), nd, nl)[:width]
        else:
            outer = summed[:width] / hdiag[None, :block]
        image = scale * outer + damping * direction
        alpha = rho / jnp.sum(direction * image, axis=0)
        solution = solution + alpha * direction
        resid = resid - alpha * image
        precond = resid / diag_rows
        fresh = jnp.sum(resid * precond, axis=0)
        direction = precond + fresh / rho * direction
        rho = fresh
    top = 0.5 * (solution[:block] + solution[:block].T)
    lower = jnp.linalg.cholesky(top)
    kept, errors = prune_rows(weights, mask, lower)
    own = prune_mask.shape[0]
    label = lax.axis_index("label")
    pruned_block = lax.dynamic_slice_in_dim(kept, label * own, own, 1).T
    rest_cols = rest_weight.shape[1]
    owned = lax.dynamic_slice_in_dim(solution, block + label * rest_cols, rest_cols, 0)
    cross = jax.scipy.linalg.solve_triangular(lower, owned.T, lower=True)
    delta = lax.dot_general(
        errors,
        cross,
        (((0,), (0,)), ((), ())),
        precision=lax.Precision.HIGHEST,
        preferred_element_type=jnp.float32,
    )
    updated_rest = (rest_weight.astype(jnp.float32) - delta).astype(jnp.bfloat16)
    return (pruned_block, updated_rest)


def solution(mesh):
    return jax.shard_map(
        per_device,
        mesh=mesh,
        in_specs=(
            P(("dp", "label"), None),
            P("dp", "label"),
            P("dp", "label"),
            P(("dp", "label"), None),
        ),
        out_specs=(P(("dp", "label"), None), P("dp", "label")),
        check_vma=False,
    )
```

```python
import functools

import jax
import jax.numpy as jnp
from jax import lax
from jax.experimental import pallas as pl
from jax.experimental.pallas import tpu as pltpu
from jax.sharding import PartitionSpec as P

ITERS = 6
MESH = pl.DeviceIdType.MESH

damp_fraction = 0.01
sub_width = 16


GROUPS = 16


def exchange(nd, nl, x_ref, o_ref, pbuf, sbuf, rbuf, sems, beside=None):
    psend, precv, ssend, srecv, gsend, grecv, fsend, frecv = sems
    dp = lax.axis_index("dp")
    label = lax.axis_index("label")
    core = lax.rem(dp, 2)
    chip = (dp // 2) * nl + label
    n = (nd // 2) * nl
    lanes = pbuf.shape[2]
    partner = (dp + 1 - 2 * core, label)

    def ahead(d):
        return lax.rem(chip + d, n)

    def behind(d):
        return lax.rem(chip + n - d, n)

    def device(j):
        return (2 * (j // nl) + core, lax.rem(j, nl))

    def place(half, j):
        q = half * n + j
        return (
            pl.ds(pl.multiple_of(lax.rem(q, GROUPS) * 8, 8), 8),
            pl.ds(pl.multiple_of((q // GROUPS) * lanes, 128), lanes),
        )

    def remote(src, dst, send, recv, to):
        return pltpu.make_async_remote_copy(
            src_ref=src, dst_ref=dst, send_sem=send, recv_sem=recv, device_id=to, device_id_type=MESH
        )

    def pair(d):
        return remote(x_ref.at[place(1 - core, ahead(d))], pbuf.at[d], psend.at[d], precv.at[d], partner)

    def scatter(d):
        return remote(sbuf.at[d], rbuf.at[d], ssend.at[d], srecv.at[d], device(ahead(d)))

    def gather(d):
        own = o_ref.at[place(core, chip)]
        return remote(own, own, gsend.at[d], grecv.at[d], device(ahead(d)))

    def gathered(d):
        ref = o_ref.at[place(core, behind(d))]
        return remote(ref, ref, gsend.at[d], grecv.at[d], device(behind(d)))

    def forward(d):
        ref = o_ref.at[place(core, behind(d))]
        return remote(ref, ref, fsend.at[d], frecv.at[d], partner)

    def forwarded(d):
        ref = o_ref.at[place(1 - core, behind(d))]
        return remote(ref, ref, fsend.at[d], frecv.at[d], partner)

    def each(low, body, high=n):
        def step(d, carry):
            body(d)
            return carry

        lax.fori_loop(low, high, step, 0)

    def greet():
        barrier = pltpu.get_barrier_semaphore()
        pl.semaphore_signal(barrier, inc=1, device_id=partner, device_id_type=MESH)
        each(1, lambda d: pl.semaphore_signal(barrier, inc=1, device_id=device(ahead(d)), device_id_type=MESH))
        pl.semaphore_wait(barrier, n)

    def run():
        each(1, lambda d: pair(d).start())
        pair(0).start()

        def send_sum(d):
            pair(d).wait_recv()
            sbuf[d] = x_ref[place(core, ahead(d))] + pbuf[d]
            scatter(d).start()

        each(1, send_sum)
        if beside is not None:
            each(1, lambda e: [c.start() for c in beside(remote, dp, label, e, 0)], nl)
        pair(0).wait_recv()

        def add(d, acc):
            scatter(d).wait_recv()
            return acc + rbuf[d]

        o_ref[place(core, chip)] = lax.fori_loop(1, n, add, x_ref[place(core, chip)] + pbuf[0])
        each(1, lambda d: gather(d).start())
        forward(0).start()

        def pass_on(d):
            gathered(d).wait_recv()
            forward(d).start()

        each(1, pass_on)
        each(0, lambda d: forwarded(d).wait_recv())
        if beside is not None:
            each(1, lambda e: [c.wait_recv() for c in beside(remote, dp, label, e, 1)], nl)
            each(1, lambda e: [c.wait_send() for c in beside(remote, dp, label, e, 0)], nl)
        each(0, lambda d: pair(d).wait_send())
        each(1, lambda d: scatter(d).wait_send())
        each(1, lambda d: gather(d).wait_send())
        each(0, lambda d: forward(d).wait_send())

    return greet, run


def piece_lanes(width, nd, nl):
    parts = nd * nl // GROUPS
    return -(-width // (parts * 128)) * 128


def exchange_scratch(lanes, nd, nl):
    n = nd // 2 * nl
    return [pltpu.VMEM((n, 8, lanes), jnp.float32)] * 3 + [pltpu.SemaphoreType.DMA((n,))] * 8


def first_kernel(nd, nl, x_ref, w_ref, m_ref, o_ref, wg_ref, mg_ref, pbuf, sbuf, rbuf, *sems):
    wsend, wrecv, msend, mrecv = sems[8:]
    own = m_ref.shape[1]

    def beside(remote, dp, label, e, arriving):
        to = lax.rem(label + (nl - e if arriving else e), nl)
        at = to if arriving else label
        cols = (slice(None), pl.ds(pl.multiple_of(at * own, 128), own))
        return (
            remote(w_ref, wg_ref.at[at], wsend.at[e], wrecv.at[e], (dp, to)),
            remote(m_ref, mg_ref.at[cols], msend.at[e], mrecv.at[e], (dp, to)),
        )

    greet, run = exchange(nd, nl, x_ref, o_ref, pbuf, sbuf, rbuf, sems[:8], beside)
    greet()
    label = lax.axis_index("label")
    wg_ref[label] = w_ref[...]
    mg_ref[:, pl.ds(pl.multiple_of(label * own, 128), own)] = m_ref[...]
    run()


def first_sum(x, w, mask, nd, nl):
    lanes = x.shape[1] // (nd * nl // GROUPS)
    vmem = pl.BlockSpec(memory_space=pltpu.VMEM)
    return pl.pallas_call(
        functools.partial(first_kernel, nd, nl),
        out_shape=(
            jax.ShapeDtypeStruct(x.shape, jnp.float32),
            jax.ShapeDtypeStruct((nl,) + w.shape, w.dtype),
            jax.ShapeDtypeStruct((mask.shape[0], mask.shape[1] * nl), mask.dtype),
        ),
        in_specs=[vmem] * 3,
        out_specs=(vmem,) * 3,
        scratch_shapes=exchange_scratch(lanes, nd, nl) + [pltpu.SemaphoreType.DMA((nl,))] * 4,
        compiler_params=pltpu.CompilerParams(collective_id=2, has_side_effects=True, vmem_limit_bytes=40 << 20),
        name="first_sum",
    )(x, w, mask)


def two_terms(x):
    high = x.astype(jnp.bfloat16)
    low = (x - high.astype(jnp.float32)).astype(jnp.bfloat16)
    return jnp.concatenate([high, low], axis=0)


def step_kernel(
    nd, nl, scale, c_ref, diag_ref, damp_ref, d_ref, s_ref, r_ref, rho_ref,
    dn_ref, sn_ref, rn_ref, rhon_ref, x_ref, o_ref, pbuf, sbuf, rbuf, *sems
):
    block, width = d_ref.shape
    greet, run = exchange(nd, nl, x_ref, o_ref, pbuf, sbuf, rbuf, sems)
    inner = lax.dot_general(
        two_terms(d_ref[...]), c_ref[...], (((1,), (1,)), ((), ())), preferred_element_type=jnp.float32
    )
    inner = two_terms(inner[:block] + inner[block:])
    tile = width // 3
    for begin in range(0, width, tile):
        cols = pl.ds(begin, tile)
        outer = jnp.dot(inner, c_ref[:, cols], preferred_element_type=jnp.float32)
        x_ref[:, cols] = outer[:block] + outer[block:]
    if x_ref.shape[1] > width:
        x_ref[:, width:] = jnp.zeros((block, x_ref.shape[1] - width), jnp.float32)
    greet()
    run()

    def update(g, carry):
        rows = pl.ds(pl.multiple_of(g * 8, 8), 8)
        direction = d_ref[rows, :]
        rho = rho_ref[rows, :]
        image = scale * o_ref[rows, :width] + damp_ref[...] * direction
        alpha = rho / jnp.sum(direction * image, axis=1, keepdims=True)
        sn_ref[rows, :] = s_ref[rows, :] + alpha * direction
        resid = r_ref[rows, :] - alpha * image
        precond = resid / diag_ref[...]
        fresh = jnp.sum(resid * precond, axis=1, keepdims=True)
        rn_ref[rows, :] = resid
        dn_ref[rows, :] = precond + fresh / rho * direction
        rhon_ref[rows, :] = fresh
        return carry

    lax.fori_loop(0, block // 8, update, 0)


def one_step(calib, diag, damping, state, scale, nd, nl):
    block, width = state[0].shape
    lanes = piece_lanes(width + block, nd, nl)
    padded = (block, lanes * (nd * nl // GROUPS))
    vmem = pl.BlockSpec(memory_space=pltpu.VMEM)
    return pl.pallas_call(
        functools.partial(step_kernel, nd, nl, scale),
        out_shape=tuple(jax.ShapeDtypeStruct(x.shape, jnp.float32) for x in state),
        in_specs=[vmem] * 7,
        out_specs=(vmem,) * 4,
        scratch_shapes=[pltpu.VMEM(padded, jnp.float32)] * 2 + exchange_scratch(lanes, nd, nl),
        compiler_params=pltpu.CompilerParams(collective_id=0, has_side_effects=True, vmem_limit_bytes=48 << 20),
        name="one_step",
    )(calib, diag, damping, *state)


def small_kernel(nd, nl, x_ref, o_ref, buf, send, recv):
    n = nd * nl
    me = lax.axis_index("dp") * nl + lax.axis_index("label")

    def device(j):
        return (j // nl, lax.rem(j, nl))

    def out(d):
        return pltpu.make_async_remote_copy(
            src_ref=x_ref,
            dst_ref=buf.at[me],
            send_sem=send.at[d],
            recv_sem=recv.at[d],
            device_id=device(lax.rem(me + d, n)),
            device_id_type=MESH,
        )

    def arrived(d):
        j = lax.rem(me + n - d, n)
        return pltpu.make_async_remote_copy(
            src_ref=x_ref,
            dst_ref=buf.at[j],
            send_sem=send.at[d],
            recv_sem=recv.at[d],
            device_id=device(j),
            device_id_type=MESH,
        )

    def each(body):
        def step(d, carry):
            body(d)
            return carry

        lax.fori_loop(1, n, step, 0)

    barrier = pltpu.get_barrier_semaphore()
    each(lambda d: pl.semaphore_signal(barrier, inc=1, device_id=device(lax.rem(me + d, n)), device_id_type=MESH))
    pl.semaphore_wait(barrier, n - 1)
    each(lambda d: out(d).start())
    buf[me] = x_ref[...]
    each(lambda d: arrived(d).wait_recv())
    o_ref[...] = lax.fori_loop(1, n, lambda j, acc: acc + buf[j], buf[0])
    each(lambda d: out(d).wait_send())


def small_sum(x, nd, nl):
    n = nd * nl
    return pl.pallas_call(
        functools.partial(small_kernel, nd, nl),
        out_shape=jax.ShapeDtypeStruct(x.shape, jnp.float32),
        in_specs=[pl.BlockSpec(memory_space=pltpu.VMEM)],
        out_specs=pl.BlockSpec(memory_space=pltpu.VMEM),
        scratch_shapes=[
            pltpu.VMEM((n,) + x.shape, jnp.float32),
            pltpu.SemaphoreType.DMA((n,)),
            pltpu.SemaphoreType.DMA((n,)),
        ],
        compiler_params=pltpu.CompilerParams(collective_id=1, has_side_effects=True),
        name="small_sum",
    )(x)


def prune_kernel(w_ref, m_ref, l_ref, kept_ref, err_ref):
    block = w_ref.shape[0]
    err_ref[...] = jnp.zeros_like(err_ref)
    for begin in range(0, block, sub_width):
        rows = pl.ds(begin, sub_width)
        window = w_ref[rows, :].astype(jnp.float32)
        chosen = m_ref[rows, :].astype(jnp.float32)
        factor = l_ref[rows, :]
        if begin:
            window = window - jnp.dot(
                factor, err_ref[...], precision=lax.Precision.HIGHEST, preferred_element_type=jnp.float32
            )
        for offset in range(sub_width):
            index = begin + offset
            column = factor[:, index : index + 1]
            inverse = 1.0 / factor[offset : offset + 1, index : index + 1]
            error = chosen[offset : offset + 1, :] * window[offset : offset + 1, :] * inverse
            err_ref[index : index + 1, :] = error
            window = window - column * error
        kept_ref[rows, :] = ((1.0 - chosen) * window).astype(kept_ref.dtype)


def prune_rows(weights, mask, lower):
    block, rows = weights.shape
    tile = min(rows, 2048)
    spec = pl.BlockSpec((block, tile), lambda i: (0, i))
    return pl.pallas_call(
        prune_kernel,
        grid=(rows // tile,),
        out_shape=(
            jax.ShapeDtypeStruct((block, rows), jnp.bfloat16),
            jax.ShapeDtypeStruct((block, rows), jnp.float32),
        ),
        in_specs=[spec, spec, pl.BlockSpec((block, block), lambda i: (0, 0))],
        out_specs=(spec, spec),
        compiler_params=pltpu.CompilerParams(vmem_limit_bytes=32 << 20),
        name="prune_rows",
    )(weights, mask, lower)


def per_device(calib, block_weight, rest_weight, prune_mask):
    tokens = calib.shape[0]
    width = calib.shape[1]
    block = prune_mask.shape[1]
    nd, nl = lax.axis_size("dp"), lax.axis_size("label")
    total = tokens * nd * nl
    stat_rows = width // block
    padded = piece_lanes(width + block, nd, nl) * (nd * nl // GROUPS)
    local_sq = jnp.sum(jnp.square(calib.astype(jnp.float32)), axis=0)
    first = lax.dot_general(
        calib[:, :block], calib, (((0,), (0,)), ((), ())), preferred_element_type=jnp.float32
    )
    stats = jnp.pad(local_sq.reshape(stat_rows, block), ((0, block - stat_rows), (0, padded - width - block)))
    summed, weights, mask = first_sum(
        jnp.concatenate([first, stats], axis=1), block_weight.T, prune_mask.T.astype(jnp.bfloat16), nd, nl
    )
    weights = weights.reshape(block, -1)
    colsq = summed[:stat_rows, width : width + block].reshape(1, width)
    damping = damp_fraction * 2.0 * jnp.sum(colsq) / (total * width)
    scale = 2.0 / total
    diag = scale * colsq + damping
    resid = jnp.eye(block, width, dtype=jnp.float32)
    precond = resid / diag
    direction = precond
    rho = jnp.sum(resid * precond, axis=1, keepdims=True)
    image = scale * (summed[:, :width] / diag[:, :block].T) + damping * direction
    alpha = rho / jnp.sum(direction * image, axis=1, keepdims=True)
    solution = alpha * direction
    resid = resid - alpha * image
    precond = resid / diag
    fresh = jnp.sum(resid * precond, axis=1, keepdims=True)
    direction = precond + fresh / rho * direction
    state = (direction, solution, resid, fresh)
    for step in range(1, ITERS - 1):
        state = one_step(calib, diag, damping.reshape(1, 1), state, scale, nd, nl)
    direction, solution, resid, rho = state
    inner = jnp.einsum(
        "bk,tk->bt", direction, calib, precision=lax.Precision.HIGHEST, preferred_element_type=jnp.float32
    )
    local = jnp.pad(jnp.sum(inner * inner, axis=1)[None, :], ((0, 7), (0, 0)))
    energy = scale * small_sum(local, nd, nl)[0] + damping * jnp.sum(direction * direction, axis=1)
    solution = solution + rho / energy[:, None] * direction
    top = 0.5 * (solution[:, :block] + solution[:, :block].T)
    lower = jnp.linalg.cholesky(top)
    kept, errors = prune_rows(weights, mask, lower)
    own = prune_mask.shape[0]
    label = lax.axis_index("label")
    pruned_block = lax.dynamic_slice_in_dim(kept, label * own, own, 1).T
    rest_cols = rest_weight.shape[1]
    owned = lax.dynamic_slice_in_dim(solution, block + label * rest_cols, rest_cols, 1)
    cross = jax.scipy.linalg.solve_triangular(lower, owned, lower=True)
    delta = lax.dot_general(
        errors,
        cross,
        (((0,), (0,)), ((), ())),
        precision=lax.Precision.HIGHEST,
        preferred_element_type=jnp.float32,
    )
    updated_rest = (rest_weight.astype(jnp.float32) - delta).astype(jnp.bfloat16)
    return (pruned_block, updated_rest)


def solution(mesh):
    return jax.shard_map(
        per_device,
        mesh=mesh,
        in_specs=(
            P(("dp", "label"), None),
            P("dp", "label"),
            P("dp", "label"),
            P(("dp", "label"), None),
        ),
        out_specs=(P(("dp", "label"), None), P("dp", "label")),
        check_vma=False,
    )
```

```python
import functools

import jax
import jax.numpy as jnp
from jax import lax
from jax.experimental import pallas as pl
from jax.experimental.pallas import tpu as pltpu
from jax.sharding import PartitionSpec as P

ITERS = 6
MESH = pl.DeviceIdType.MESH

damp_fraction = 0.01
sub_width = 16


GROUPS = 16


def exchange(nd, nl, x_ref, o_ref, pbuf, sbuf, rbuf, sems, beside=None):
    psend, precv, ssend, srecv, gsend, grecv, fsend, frecv = sems
    dp = lax.axis_index("dp")
    label = lax.axis_index("label")
    core = lax.rem(dp, 2)
    chip = (dp // 2) * nl + label
    n = (nd // 2) * nl
    lanes = pbuf.shape[2]
    partner = (dp + 1 - 2 * core, label)

    def ahead(d):
        return lax.rem(chip + d, n)

    def behind(d):
        return lax.rem(chip + n - d, n)

    def device(j):
        return (2 * (j // nl) + core, lax.rem(j, nl))

    def place(half, j):
        q = half * n + j
        return (
            pl.ds(pl.multiple_of(lax.rem(q, GROUPS) * 8, 8), 8),
            pl.ds(pl.multiple_of((q // GROUPS) * lanes, 128), lanes),
        )

    def remote(src, dst, send, recv, to):
        return pltpu.make_async_remote_copy(
            src_ref=src, dst_ref=dst, send_sem=send, recv_sem=recv, device_id=to, device_id_type=MESH
        )

    def pair(d):
        return remote(x_ref.at[place(1 - core, ahead(d))], pbuf.at[d], psend.at[d], precv.at[d], partner)

    def scatter(d):
        return remote(sbuf.at[d], rbuf.at[d], ssend.at[d], srecv.at[d], device(ahead(d)))

    def gather(d):
        own = o_ref.at[place(core, chip)]
        return remote(own, own, gsend.at[d], grecv.at[d], device(ahead(d)))

    def gathered(d):
        ref = o_ref.at[place(core, behind(d))]
        return remote(ref, ref, gsend.at[d], grecv.at[d], device(behind(d)))

    def forward(d):
        ref = o_ref.at[place(core, behind(d))]
        return remote(ref, ref, fsend.at[d], frecv.at[d], partner)

    def forwarded(d):
        ref = o_ref.at[place(1 - core, behind(d))]
        return remote(ref, ref, fsend.at[d], frecv.at[d], partner)

    def each(low, body, high=n):
        def step(d, carry):
            body(d)
            return carry

        lax.fori_loop(low, high, step, 0)

    def greet():
        barrier = pltpu.get_barrier_semaphore()
        pl.semaphore_signal(barrier, inc=1, device_id=partner, device_id_type=MESH)
        each(1, lambda d: pl.semaphore_signal(barrier, inc=1, device_id=device(ahead(d)), device_id_type=MESH))
        pl.semaphore_wait(barrier, n)

    def run():
        each(1, lambda d: pair(d).start())
        pair(0).start()

        def send_sum(d):
            pair(d).wait_recv()
            sbuf[d] = x_ref[place(core, ahead(d))] + pbuf[d]
            scatter(d).start()

        each(1, send_sum)
        if beside is not None:
            each(1, lambda e: [c.start() for c in beside(remote, dp, label, e, 0)], nl)
        pair(0).wait_recv()

        def add(d, acc):
            scatter(d).wait_recv()
            return acc + rbuf[d]

        o_ref[place(core, chip)] = lax.fori_loop(1, n, add, x_ref[place(core, chip)] + pbuf[0])
        each(1, lambda d: gather(d).start())
        forward(0).start()

        def pass_on(d):
            gathered(d).wait_recv()
            forward(d).start()

        each(1, pass_on)
        each(0, lambda d: forwarded(d).wait_recv())
        if beside is not None:
            each(1, lambda e: [c.wait_recv() for c in beside(remote, dp, label, e, 1)], nl)
            each(1, lambda e: [c.wait_send() for c in beside(remote, dp, label, e, 0)], nl)
        each(0, lambda d: pair(d).wait_send())
        each(1, lambda d: scatter(d).wait_send())
        each(1, lambda d: gather(d).wait_send())
        each(0, lambda d: forward(d).wait_send())

    return greet, run


def piece_lanes(width, nd, nl):
    parts = nd * nl // GROUPS
    return -(-width // (parts * 128)) * 128


def exchange_scratch(lanes, nd, nl):
    n = nd // 2 * nl
    return [pltpu.VMEM((n, 8, lanes), jnp.float32)] * 3 + [pltpu.SemaphoreType.DMA((n,))] * 8


def first_kernel(nd, nl, x_ref, w_ref, m_ref, o_ref, wg_ref, mg_ref, pbuf, sbuf, rbuf, *sems):
    wsend, wrecv, msend, mrecv = sems[8:]
    own = m_ref.shape[1]

    def beside(remote, dp, label, e, arriving):
        to = lax.rem(label + (nl - e if arriving else e), nl)
        at = to if arriving else label
        cols = (slice(None), pl.ds(pl.multiple_of(at * own, 128), own))
        return (
            remote(w_ref, wg_ref.at[at], wsend.at[e], wrecv.at[e], (dp, to)),
            remote(m_ref, mg_ref.at[cols], msend.at[e], mrecv.at[e], (dp, to)),
        )

    greet, run = exchange(nd, nl, x_ref, o_ref, pbuf, sbuf, rbuf, sems[:8], beside)
    greet()
    label = lax.axis_index("label")
    wg_ref[label] = w_ref[...]
    mg_ref[:, pl.ds(pl.multiple_of(label * own, 128), own)] = m_ref[...]
    run()


def first_sum(x, w, mask, nd, nl):
    lanes = x.shape[1] // (nd * nl // GROUPS)
    vmem = pl.BlockSpec(memory_space=pltpu.VMEM)
    return pl.pallas_call(
        functools.partial(first_kernel, nd, nl),
        out_shape=(
            jax.ShapeDtypeStruct(x.shape, jnp.float32),
            jax.ShapeDtypeStruct((nl,) + w.shape, w.dtype),
            jax.ShapeDtypeStruct((mask.shape[0], mask.shape[1] * nl), mask.dtype),
        ),
        in_specs=[vmem] * 3,
        out_specs=(vmem,) * 3,
        scratch_shapes=exchange_scratch(lanes, nd, nl) + [pltpu.SemaphoreType.DMA((nl,))] * 4,
        compiler_params=pltpu.CompilerParams(collective_id=2, has_side_effects=True, vmem_limit_bytes=40 << 20),
        name="first_sum",
    )(x, w, mask)


def two_terms(x):
    high = x.astype(jnp.bfloat16)
    low = (x - high.astype(jnp.float32)).astype(jnp.bfloat16)
    return jnp.concatenate([high, low], axis=0)


def steps_kernel(
    nd, nl, scale, steps, c_ref, diag_ref, damp_ref, d0_ref, s0_ref, r0_ref, rho0_ref,
    d_ref, s_ref, rho_ref, local_ref, r_ref, x_ref, o_ref, pbuf, sbuf, rbuf, *sems
):
    block, width = d_ref.shape
    greet, run = exchange(nd, nl, x_ref, o_ref, pbuf, sbuf, rbuf, sems)
    d_ref[...] = d0_ref[...]
    s_ref[...] = s0_ref[...]
    r_ref[...] = r0_ref[...]
    rho_ref[...] = rho0_ref[...]
    if x_ref.shape[1] > width:
        x_ref[:, width:] = jnp.zeros((block, x_ref.shape[1] - width), jnp.float32)
    tile = width // 3
    greet()

    def project():
        inner = lax.dot_general(
            two_terms(d_ref[...]), c_ref[...], (((1,), (1,)), ((), ())), preferred_element_type=jnp.float32
        )
        return inner[:block] + inner[block:]

    def update(g, carry):
        rows = pl.ds(pl.multiple_of(g * 8, 8), 8)
        direction = d_ref[rows, :]
        rho = rho_ref[rows, :]
        image = scale * o_ref[rows, :width] + damp_ref[...] * direction
        alpha = rho / jnp.sum(direction * image, axis=1, keepdims=True)
        s_ref[rows, :] = s_ref[rows, :] + alpha * direction
        resid = r_ref[rows, :] - alpha * image
        precond = resid / diag_ref[...]
        fresh = jnp.sum(resid * precond, axis=1, keepdims=True)
        r_ref[rows, :] = resid
        d_ref[rows, :] = precond + fresh / rho * direction
        rho_ref[rows, :] = fresh
        return carry

    def step(index, carry):
        inner = two_terms(project())
        for begin in range(0, width, tile):
            cols = pl.ds(begin, tile)
            outer = jnp.dot(inner, c_ref[:, cols], preferred_element_type=jnp.float32)
            x_ref[:, cols] = outer[:block] + outer[block:]
        run()
        lax.fori_loop(0, block // 8, update, 0)
        return carry

    lax.fori_loop(0, steps, step, 0)
    inner = project()
    local_ref[...] = lax.dot_general(
        jnp.ones((8, inner.shape[1]), jnp.float32),
        inner * inner,
        (((1,), (1,)), ((), ())),
        precision=lax.Precision.HIGHEST,
        preferred_element_type=jnp.float32,
    )


def middle_steps(calib, diag, damping, state, scale, steps, nd, nl):
    block, width = state[0].shape
    lanes = piece_lanes(width + block, nd, nl)
    padded = (block, lanes * (nd * nl // GROUPS))
    vmem = pl.BlockSpec(memory_space=pltpu.VMEM)
    whole = jax.ShapeDtypeStruct((block, width), jnp.float32)
    return pl.pallas_call(
        functools.partial(steps_kernel, nd, nl, scale, steps),
        out_shape=(
            whole,
            whole,
            jax.ShapeDtypeStruct((block, 1), jnp.float32),
            jax.ShapeDtypeStruct((8, block), jnp.float32),
        ),
        in_specs=[vmem] * 7,
        out_specs=(vmem,) * 4,
        scratch_shapes=[pltpu.VMEM((block, width), jnp.float32)]
        + [pltpu.VMEM(padded, jnp.float32)] * 2
        + exchange_scratch(lanes, nd, nl),
        compiler_params=pltpu.CompilerParams(collective_id=0, has_side_effects=True, vmem_limit_bytes=52 << 20),
        name="middle_steps",
    )(calib, diag, damping, *state)


def small_kernel(nd, nl, x_ref, o_ref, buf, send, recv):
    n = nd * nl
    me = lax.axis_index("dp") * nl + lax.axis_index("label")

    def device(j):
        return (j // nl, lax.rem(j, nl))

    def out(d):
        return pltpu.make_async_remote_copy(
            src_ref=x_ref,
            dst_ref=buf.at[me],
            send_sem=send.at[d],
            recv_sem=recv.at[d],
            device_id=device(lax.rem(me + d, n)),
            device_id_type=MESH,
        )

    def arrived(d):
        j = lax.rem(me + n - d, n)
        return pltpu.make_async_remote_copy(
            src_ref=x_ref,
            dst_ref=buf.at[j],
            send_sem=send.at[d],
            recv_sem=recv.at[d],
            device_id=device(j),
            device_id_type=MESH,
        )

    def each(body):
        def step(d, carry):
            body(d)
            return carry

        lax.fori_loop(1, n, step, 0)

    barrier = pltpu.get_barrier_semaphore()
    each(lambda d: pl.semaphore_signal(barrier, inc=1, device_id=device(lax.rem(me + d, n)), device_id_type=MESH))
    pl.semaphore_wait(barrier, n - 1)
    each(lambda d: out(d).start())
    buf[me] = x_ref[...]
    each(lambda d: arrived(d).wait_recv())
    o_ref[...] = lax.fori_loop(1, n, lambda j, acc: acc + buf[j], buf[0])
    each(lambda d: out(d).wait_send())


def small_sum(x, nd, nl):
    n = nd * nl
    return pl.pallas_call(
        functools.partial(small_kernel, nd, nl),
        out_shape=jax.ShapeDtypeStruct(x.shape, jnp.float32),
        in_specs=[pl.BlockSpec(memory_space=pltpu.VMEM)],
        out_specs=pl.BlockSpec(memory_space=pltpu.VMEM),
        scratch_shapes=[
            pltpu.VMEM((n,) + x.shape, jnp.float32),
            pltpu.SemaphoreType.DMA((n,)),
            pltpu.SemaphoreType.DMA((n,)),
        ],
        compiler_params=pltpu.CompilerParams(collective_id=1, has_side_effects=True),
        name="small_sum",
    )(x)


def prune_kernel(w_ref, m_ref, l_ref, t_ref, kept_ref, err_ref, cross_ref):
    block = w_ref.shape[0]
    err_ref[...] = jnp.zeros_like(err_ref)
    cross_ref[...] = jnp.zeros_like(cross_ref)

    def earlier(factor, ref):
        return jnp.dot(factor, ref[...], precision=lax.Precision.HIGHEST, preferred_element_type=jnp.float32)

    for begin in range(0, block, sub_width):
        rows = pl.ds(begin, sub_width)
        window = w_ref[rows, :].astype(jnp.float32)
        target = t_ref[rows, :]
        chosen = m_ref[rows, :].astype(jnp.float32)
        factor = l_ref[rows, :]
        if begin:
            window = window - earlier(factor, err_ref)
            target = target - earlier(factor, cross_ref)
        for offset in range(sub_width):
            index = begin + offset
            one = slice(offset, offset + 1)
            column = factor[:, index : index + 1]
            inverse = 1.0 / factor[one, index : index + 1]
            error = chosen[one, :] * window[one, :] * inverse
            solved = target[one, :] * inverse
            err_ref[index : index + 1, :] = error
            cross_ref[index : index + 1, :] = solved
            window = window - column * error
            target = target - column * solved
        kept_ref[rows, :] = ((1.0 - chosen) * window).astype(kept_ref.dtype)


def prune_rows(weights, mask, lower, target):
    block, rows = weights.shape
    tile = min(rows, 2048)
    spec = pl.BlockSpec((block, tile), lambda i: (0, i))
    fixed = [pl.BlockSpec(x.shape, lambda i: (0, 0)) for x in (lower, target)]
    return pl.pallas_call(
        prune_kernel,
        grid=(rows // tile,),
        out_shape=(
            jax.ShapeDtypeStruct((block, rows), jnp.bfloat16),
            jax.ShapeDtypeStruct((block, rows), jnp.float32),
            jax.ShapeDtypeStruct(target.shape, jnp.float32),
        ),
        in_specs=[spec, spec] + fixed,
        out_specs=(spec, spec, fixed[1]),
        compiler_params=pltpu.CompilerParams(vmem_limit_bytes=32 << 20),
        name="prune_rows",
    )(weights, mask, lower, target)


def per_device(calib, block_weight, rest_weight, prune_mask):
    tokens = calib.shape[0]
    width = calib.shape[1]
    block = prune_mask.shape[1]
    nd, nl = lax.axis_size("dp"), lax.axis_size("label")
    total = tokens * nd * nl
    stat_rows = width // block
    padded = piece_lanes(width + block, nd, nl) * (nd * nl // GROUPS)
    local_sq = jnp.sum(jnp.square(calib.astype(jnp.float32)), axis=0)
    first = lax.dot_general(
        calib[:, :block], calib, (((0,), (0,)), ((), ())), preferred_element_type=jnp.float32
    )
    stats = jnp.pad(local_sq.reshape(stat_rows, block), ((0, block - stat_rows), (0, padded - width - block)))
    summed, weights, mask = first_sum(
        jnp.concatenate([first, stats], axis=1), block_weight.T, prune_mask.T.astype(jnp.bfloat16), nd, nl
    )
    weights = weights.reshape(block, -1)
    colsq = summed[:stat_rows, width : width + block].reshape(1, width)
    damping = damp_fraction * 2.0 * jnp.sum(colsq) / (total * width)
    scale = 2.0 / total
    diag = scale * colsq + damping
    resid = jnp.eye(block, width, dtype=jnp.float32)
    precond = resid / diag
    direction = precond
    rho = jnp.sum(resid * precond, axis=1, keepdims=True)
    image = scale * (summed[:, :width] / diag[:, :block].T) + damping * direction
    alpha = rho / jnp.sum(direction * image, axis=1, keepdims=True)
    solution = alpha * direction
    resid = resid - alpha * image
    precond = resid / diag
    fresh = jnp.sum(resid * precond, axis=1, keepdims=True)
    direction = precond + fresh / rho * direction
    state = (direction, solution, resid, fresh)
    direction, solution, rho, local = middle_steps(
        calib, diag, damping.reshape(1, 1), state, scale, ITERS - 2, nd, nl
    )
    energy = scale * small_sum(local, nd, nl)[0] + damping * jnp.sum(direction * direction, axis=1)
    solution = solution + rho / energy[:, None] * direction
    top = 0.5 * (solution[:, :block] + solution[:, :block].T)
    lower = jnp.linalg.cholesky(top)
    own = prune_mask.shape[0]
    label = lax.axis_index("label")
    rest_cols = rest_weight.shape[1]
    owned = lax.dynamic_slice_in_dim(solution, block + label * rest_cols, rest_cols, 1)
    kept, errors, cross = prune_rows(weights, mask, lower, owned)
    pruned_block = lax.dynamic_slice_in_dim(kept, label * own, own, 1).T
    delta = lax.dot_general(
        errors,
        cross,
        (((0,), (0,)), ((), ())),
        precision=lax.Precision.HIGHEST,
        preferred_element_type=jnp.float32,
    )
    updated_rest = (rest_weight.astype(jnp.float32) - delta).astype(jnp.bfloat16)
    return (pruned_block, updated_rest)


def solution(mesh):
    return jax.shard_map(
        per_device,
        mesh=mesh,
        in_specs=(
            P(("dp", "label"), None),
            P("dp", "label"),
            P("dp", "label"),
            P(("dp", "label"), None),
        ),
        out_specs=(P(("dp", "label"), None), P("dp", "label")),
        check_vma=False,
    )
```

```python
import functools

import jax
import jax.numpy as jnp
from jax import lax
from jax.experimental import pallas as pl
from jax.experimental.pallas import tpu as pltpu
from jax.sharding import PartitionSpec as P

ITERS = 6
MESH = pl.DeviceIdType.MESH

damp_fraction = 0.01
sub_width = 16


GROUPS = 16


def exchange(nd, nl, x_ref, o_ref, pbuf, sbuf, rbuf, sems):
    psend, precv, ssend, srecv, gsend, grecv, fsend, frecv = sems
    dp = lax.axis_index("dp")
    label = lax.axis_index("label")
    core = lax.rem(dp, 2)
    chip = (dp // 2) * nl + label
    n = (nd // 2) * nl
    lanes = pbuf.shape[2]
    partner = (dp + 1 - 2 * core, label)

    def ahead(d):
        return lax.rem(chip + d, n)

    def behind(d):
        return lax.rem(chip + n - d, n)

    def device(j):
        return (2 * (j // nl) + core, lax.rem(j, nl))

    def place(half, j):
        q = half * n + j
        return (
            pl.ds(pl.multiple_of(lax.rem(q, GROUPS) * 8, 8), 8),
            pl.ds(pl.multiple_of((q // GROUPS) * lanes, 128), lanes),
        )

    def remote(src, dst, send, recv, to):
        return pltpu.make_async_remote_copy(
            src_ref=src, dst_ref=dst, send_sem=send, recv_sem=recv, device_id=to, device_id_type=MESH
        )

    def pair(d):
        return remote(x_ref.at[place(1 - core, ahead(d))], pbuf.at[d], psend.at[d], precv.at[d], partner)

    def scatter(d):
        return remote(sbuf.at[d], rbuf.at[d], ssend.at[d], srecv.at[d], device(ahead(d)))

    def gather(d):
        own = o_ref.at[place(core, chip)]
        return remote(own, own, gsend.at[d], grecv.at[d], device(ahead(d)))

    def gathered(d):
        ref = o_ref.at[place(core, behind(d))]
        return remote(ref, ref, gsend.at[d], grecv.at[d], device(behind(d)))

    def forward(d):
        ref = o_ref.at[place(core, behind(d))]
        return remote(ref, ref, fsend.at[d], frecv.at[d], partner)

    def forwarded(d):
        ref = o_ref.at[place(1 - core, behind(d))]
        return remote(ref, ref, fsend.at[d], frecv.at[d], partner)

    def each(low, body, high=n):
        def step(d, carry):
            body(d)
            return carry

        lax.fori_loop(low, high, step, 0)

    def greet():
        barrier = pltpu.get_barrier_semaphore()
        pl.semaphore_signal(barrier, inc=1, device_id=partner, device_id_type=MESH)
        each(1, lambda d: pl.semaphore_signal(barrier, inc=1, device_id=device(ahead(d)), device_id_type=MESH))
        pl.semaphore_wait(barrier, n)

    def run():
        each(1, lambda d: pair(d).start())
        pair(0).start()

        def send_sum(d):
            pair(d).wait_recv()
            sbuf[d] = x_ref[place(core, ahead(d))] + pbuf[d]
            scatter(d).start()

        each(1, send_sum)
        pair(0).wait_recv()

        def add(d, acc):
            scatter(d).wait_recv()
            return acc + rbuf[d]

        o_ref[place(core, chip)] = lax.fori_loop(1, n, add, x_ref[place(core, chip)] + pbuf[0])
        each(1, lambda d: gather(d).start())
        forward(0).start()

        def pass_on(d):
            gathered(d).wait_recv()
            forward(d).start()

        each(1, pass_on)
        each(0, lambda d: forwarded(d).wait_recv())
        each(0, lambda d: pair(d).wait_send())
        each(1, lambda d: scatter(d).wait_send())
        each(1, lambda d: gather(d).wait_send())
        each(0, lambda d: forward(d).wait_send())

    def energy(local_ref, part, slots, sums):
        esend, erecv, csend, crecv = sums
        near = remote(local_ref, part, esend, erecv, partner)
        near.start()
        near.wait_recv()
        slots[chip] = local_ref[...] + part[...]

        def far(d, j):
            return remote(slots.at[j], slots.at[j], csend.at[d], crecv.at[d], device(ahead(d)))

        each(1, lambda d: far(d, chip).start())
        each(1, lambda d: far(d, behind(d)).wait_recv())
        near.wait_send()
        each(1, lambda d: far(d, chip).wait_send())
        return lax.fori_loop(1, n, lambda j, acc: acc + slots[j], slots[0])

    return greet, run, energy, remote, each


def piece_lanes(width, nd, nl):
    parts = nd * nl // GROUPS
    return -(-width // (parts * 128)) * 128


def exchange_scratch(lanes, nd, nl):
    n = nd // 2 * nl
    return [pltpu.VMEM((n, 8, lanes), jnp.float32)] * 3 + [pltpu.SemaphoreType.DMA((n,))] * 8


def first_kernel(nd, nl, x_ref, o_ref, pbuf, sbuf, rbuf, *sems):
    greet, run = exchange(nd, nl, x_ref, o_ref, pbuf, sbuf, rbuf, sems)[:2]
    greet()
    run()


def first_sum(x, nd, nl):
    lanes = x.shape[1] // (nd * nl // GROUPS)
    vmem = pl.BlockSpec(memory_space=pltpu.VMEM)
    return pl.pallas_call(
        functools.partial(first_kernel, nd, nl),
        out_shape=jax.ShapeDtypeStruct(x.shape, jnp.float32),
        in_specs=[vmem],
        out_specs=vmem,
        scratch_shapes=exchange_scratch(lanes, nd, nl),
        compiler_params=pltpu.CompilerParams(collective_id=2, has_side_effects=True, vmem_limit_bytes=40 << 20),
        name="first_sum",
    )(x)


def two_terms(x):
    high = x.astype(jnp.bfloat16)
    low = (x - high.astype(jnp.float32)).astype(jnp.bfloat16)
    return jnp.concatenate([high, low], axis=0)


def steps_kernel(
    nd, nl, scale, steps, c_ref, diag_ref, damp_ref, d0_ref, s0_ref, r0_ref, rho0_ref, w_ref, m_ref,
    d_ref, s_ref, rho_ref, energy_ref, wg_ref, mg_ref, r_ref, local_ref, part, slots, x_ref, o_ref,
    pbuf, sbuf, rbuf, *sems
):
    block, width = d_ref.shape
    greet, run, energy, remote, each = exchange(nd, nl, x_ref, o_ref, pbuf, sbuf, rbuf, sems[:8])
    wsend, wrecv, msend, mrecv = sems[8:12]
    dp = lax.axis_index("dp")
    label = lax.axis_index("label")
    own = m_ref.shape[1]
    share = -(-(nl - 1) // steps)

    def columns(at):
        return (slice(None), pl.ds(pl.multiple_of(at * own, 128), own))

    def beside(e, arriving):
        to = lax.rem(label + (nl - e if arriving else e), nl)
        at = to if arriving else label
        return (
            remote(w_ref, wg_ref.at[at], wsend.at[e], wrecv.at[e], (dp, to)),
            remote(m_ref, mg_ref.at[columns(at)], msend.at[e], mrecv.at[e], (dp, to)),
        )

    wg_ref[label] = w_ref[...]
    mg_ref[columns(label)] = m_ref[...]
    d_ref[...] = d0_ref[...]
    s_ref[...] = s0_ref[...]
    r_ref[...] = r0_ref[...]
    rho_ref[...] = rho0_ref[...]
    if x_ref.shape[1] > width:
        x_ref[:, width:] = jnp.zeros((block, x_ref.shape[1] - width), jnp.float32)
    tile = width // 3
    greet()

    def project():
        inner = lax.dot_general(
            two_terms(d_ref[...]), c_ref[...], (((1,), (1,)), ((), ())), preferred_element_type=jnp.float32
        )
        return inner[:block] + inner[block:]

    def update(g, carry):
        rows = pl.ds(pl.multiple_of(g * 8, 8), 8)
        direction = d_ref[rows, :]
        rho = rho_ref[rows, :]
        image = scale * o_ref[rows, :width] + damp_ref[...] * direction
        alpha = rho / jnp.sum(direction * image, axis=1, keepdims=True)
        s_ref[rows, :] = s_ref[rows, :] + alpha * direction
        resid = r_ref[rows, :] - alpha * image
        precond = resid / diag_ref[...]
        fresh = jnp.sum(resid * precond, axis=1, keepdims=True)
        r_ref[rows, :] = resid
        d_ref[rows, :] = precond + fresh / rho * direction
        rho_ref[rows, :] = fresh
        return carry

    def step(index, carry):
        first = 1 + index * share

        def send(e, carry):
            for copy in beside(e, False):
                copy.start()
            return carry

        lax.fori_loop(first, jnp.minimum(first + share, nl), send, 0)
        inner = two_terms(project())
        for begin in range(0, width, tile):
            cols = pl.ds(begin, tile)
            outer = jnp.dot(inner, c_ref[:, cols], preferred_element_type=jnp.float32)
            x_ref[:, cols] = outer[:block] + outer[block:]
        run()
        lax.fori_loop(0, block // 8, update, 0)
        return carry

    lax.fori_loop(0, steps, step, 0)
    inner = project()
    local_ref[...] = lax.dot_general(
        jnp.ones((8, inner.shape[1]), jnp.float32),
        inner * inner,
        (((1,), (1,)), ((), ())),
        precision=lax.Precision.HIGHEST,
        preferred_element_type=jnp.float32,
    )
    energy_ref[...] = energy(local_ref, part, slots, sems[12:])
    each(1, lambda e: [copy.wait_recv() for copy in beside(e, True)], nl)
    each(1, lambda e: [copy.wait_send() for copy in beside(e, False)], nl)


def middle_steps(calib, diag, damping, state, w, mask, scale, steps, nd, nl):
    block, width = state[0].shape
    lanes = piece_lanes(width + block, nd, nl)
    n = nd // 2 * nl
    padded = (block, lanes * (nd * nl // GROUPS))
    vmem = pl.BlockSpec(memory_space=pltpu.VMEM)
    whole = jax.ShapeDtypeStruct((block, width), jnp.float32)
    return pl.pallas_call(
        functools.partial(steps_kernel, nd, nl, scale, steps),
        out_shape=(
            whole,
            whole,
            jax.ShapeDtypeStruct((block, 1), jnp.float32),
            jax.ShapeDtypeStruct((8, block), jnp.float32),
            jax.ShapeDtypeStruct((nl,) + w.shape, w.dtype),
            jax.ShapeDtypeStruct((mask.shape[0], mask.shape[1] * nl), mask.dtype),
        ),
        in_specs=[vmem] * 9,
        out_specs=(vmem,) * 6,
        scratch_shapes=[pltpu.VMEM((block, width), jnp.float32)]
        + [pltpu.VMEM((8, block), jnp.float32)] * 2
        + [pltpu.VMEM((n, 8, block), jnp.float32)]
        + [pltpu.VMEM(padded, jnp.float32)] * 2
        + exchange_scratch(lanes, nd, nl)
        + [pltpu.SemaphoreType.DMA((nl,))] * 4
        + [pltpu.SemaphoreType.DMA] * 2
        + [pltpu.SemaphoreType.DMA((n,))] * 2,
        compiler_params=pltpu.CompilerParams(collective_id=0, has_side_effects=True, vmem_limit_bytes=52 << 20),
        name="middle_steps",
    )(calib, diag, damping, *state, w, mask)


def prune_kernel(w_ref, m_ref, l_ref, t_ref, kept_ref, err_ref, cross_ref):
    block = w_ref.shape[0]
    err_ref[...] = jnp.zeros_like(err_ref)
    cross_ref[...] = jnp.zeros_like(cross_ref)

    def earlier(factor, ref):
        return jnp.dot(factor, ref[...], precision=lax.Precision.HIGHEST, preferred_element_type=jnp.float32)

    for begin in range(0, block, sub_width):
        rows = pl.ds(begin, sub_width)
        window = w_ref[rows, :].astype(jnp.float32)
        target = t_ref[rows, :]
        chosen = m_ref[rows, :].astype(jnp.float32)
        factor = l_ref[rows, :]
        if begin:
            window = window - earlier(factor, err_ref)
            target = target - earlier(factor, cross_ref)
        for offset in range(sub_width):
            index = begin + offset
            one = slice(offset, offset + 1)
            column = factor[:, index : index + 1]
            inverse = 1.0 / factor[one, index : index + 1]
            error = chosen[one, :] * window[one, :] * inverse
            solved = target[one, :] * inverse
            err_ref[index : index + 1, :] = error
            cross_ref[index : index + 1, :] = solved
            window = window - column * error
            target = target - column * solved
        kept_ref[rows, :] = ((1.0 - chosen) * window).astype(kept_ref.dtype)


def prune_rows(weights, mask, lower, target):
    block, rows = weights.shape
    tile = min(rows, 2048)
    spec = pl.BlockSpec((block, tile), lambda i: (0, i))
    fixed = [pl.BlockSpec(x.shape, lambda i: (0, 0)) for x in (lower, target)]
    return pl.pallas_call(
        prune_kernel,
        grid=(rows // tile,),
        out_shape=(
            jax.ShapeDtypeStruct((block, rows), jnp.bfloat16),
            jax.ShapeDtypeStruct((block, rows), jnp.float32),
            jax.ShapeDtypeStruct(target.shape, jnp.float32),
        ),
        in_specs=[spec, spec] + fixed,
        out_specs=(spec, spec, fixed[1]),
        compiler_params=pltpu.CompilerParams(vmem_limit_bytes=32 << 20),
        name="prune_rows",
    )(weights, mask, lower, target)


def per_device(calib, block_weight, rest_weight, prune_mask):
    tokens = calib.shape[0]
    width = calib.shape[1]
    block = prune_mask.shape[1]
    nd, nl = lax.axis_size("dp"), lax.axis_size("label")
    total = tokens * nd * nl
    stat_rows = width // block
    padded = piece_lanes(width + block, nd, nl) * (nd * nl // GROUPS)
    local_sq = jnp.sum(jnp.square(calib.astype(jnp.float32)), axis=0)
    first = lax.dot_general(
        calib[:, :block], calib, (((0,), (0,)), ((), ())), preferred_element_type=jnp.float32
    )
    stats = jnp.pad(local_sq.reshape(stat_rows, block), ((0, block - stat_rows), (0, padded - width - block)))
    summed = first_sum(jnp.concatenate([first, stats], axis=1), nd, nl)
    colsq = summed[:stat_rows, width : width + block].reshape(1, width)
    damping = damp_fraction * 2.0 * jnp.sum(colsq) / (total * width)
    scale = 2.0 / total
    diag = scale * colsq + damping
    resid = jnp.eye(block, width, dtype=jnp.float32)
    precond = resid / diag
    direction = precond
    rho = jnp.sum(resid * precond, axis=1, keepdims=True)
    image = scale * (summed[:, :width] / diag[:, :block].T) + damping * direction
    alpha = rho / jnp.sum(direction * image, axis=1, keepdims=True)
    solution = alpha * direction
    resid = resid - alpha * image
    precond = resid / diag
    fresh = jnp.sum(resid * precond, axis=1, keepdims=True)
    direction = precond + fresh / rho * direction
    state = (direction, solution, resid, fresh)
    direction, solution, rho, norms, weights, mask = middle_steps(
        calib,
        diag,
        damping.reshape(1, 1),
        state,
        block_weight.T,
        prune_mask.T.astype(jnp.bfloat16),
        scale,
        ITERS - 2,
        nd,
        nl,
    )
    weights = weights.reshape(block, -1)
    energy = scale * norms[0] + damping * jnp.sum(direction * direction, axis=1)
    solution = solution + rho / energy[:, None] * direction
    top = 0.5 * (solution[:, :block] + solution[:, :block].T)
    lower = jnp.linalg.cholesky(top)
    own = prune_mask.shape[0]
    label = lax.axis_index("label")
    rest_cols = rest_weight.shape[1]
    owned = lax.dynamic_slice_in_dim(solution, block + label * rest_cols, rest_cols, 1)
    kept, errors, cross = prune_rows(weights, mask, lower, owned)
    pruned_block = lax.dynamic_slice_in_dim(kept, label * own, own, 1).T
    delta = lax.dot_general(
        errors,
        cross,
        (((0,), (0,)), ((), ())),
        precision=lax.Precision.HIGHEST,
        preferred_element_type=jnp.float32,
    )
    updated_rest = (rest_weight.astype(jnp.float32) - delta).astype(jnp.bfloat16)
    return (pruned_block, updated_rest)


def solution(mesh):
    return jax.shard_map(
        per_device,
        mesh=mesh,
        in_specs=(
            P(("dp", "label"), None),
            P("dp", "label"),
            P("dp", "label"),
            P(("dp", "label"), None),
        ),
        out_specs=(P(("dp", "label"), None), P("dp", "label")),
        check_vma=False,
    )
```

```python
import functools

import jax
import jax.numpy as jnp
from jax import lax
from jax.experimental import pallas as pl
from jax.experimental.pallas import tpu as pltpu
from jax.sharding import PartitionSpec as P

ITERS = 6
MESH = pl.DeviceIdType.MESH

damp_fraction = 0.01
sub_width = 16


GROUPS = 16


def exchange(nd, nl, x_ref, o_ref, pbuf, sbuf, rbuf, sems):
    psend, precv, ssend, srecv, gsend, grecv, fsend, frecv = sems
    dp = lax.axis_index("dp")
    label = lax.axis_index("label")
    core = lax.rem(dp, 2)
    chip = (dp // 2) * nl + label
    n = (nd // 2) * nl
    lanes = pbuf.shape[2]
    partner = (dp + 1 - 2 * core, label)

    def ahead(d):
        return lax.rem(chip + d, n)

    def behind(d):
        return lax.rem(chip + n - d, n)

    def device(j):
        return (2 * (j // nl) + core, lax.rem(j, nl))

    def place(half, j):
        q = half * n + j
        return (
            pl.ds(pl.multiple_of(lax.rem(q, GROUPS) * 8, 8), 8),
            pl.ds(pl.multiple_of((q // GROUPS) * lanes, 128), lanes),
        )

    def remote(src, dst, send, recv, to):
        return pltpu.make_async_remote_copy(
            src_ref=src, dst_ref=dst, send_sem=send, recv_sem=recv, device_id=to, device_id_type=MESH
        )

    def pair(d):
        return remote(x_ref.at[place(1 - core, ahead(d))], pbuf.at[d], psend.at[d], precv.at[d], partner)

    def scatter(d):
        return remote(sbuf.at[d], rbuf.at[d], ssend.at[d], srecv.at[d], device(ahead(d)))

    def gather(d):
        own = o_ref.at[place(core, chip)]
        return remote(own, own, gsend.at[d], grecv.at[d], device(ahead(d)))

    def gathered(d):
        ref = o_ref.at[place(core, behind(d))]
        return remote(ref, ref, gsend.at[d], grecv.at[d], device(behind(d)))

    def forward(d):
        ref = o_ref.at[place(core, behind(d))]
        return remote(ref, ref, fsend.at[d], frecv.at[d], partner)

    def forwarded(d):
        ref = o_ref.at[place(1 - core, behind(d))]
        return remote(ref, ref, fsend.at[d], frecv.at[d], partner)

    def each(low, body, high=n):
        def step(d, carry):
            body(d)
            return carry

        lax.fori_loop(low, high, step, 0)

    def greet():
        barrier = pltpu.get_barrier_semaphore()
        pl.semaphore_signal(barrier, inc=1, device_id=partner, device_id_type=MESH)
        each(1, lambda d: pl.semaphore_signal(barrier, inc=1, device_id=device(ahead(d)), device_id_type=MESH))
        pl.semaphore_wait(barrier, n)

    def run():
        each(1, lambda d: pair(d).start())
        pair(0).start()

        def send_sum(d):
            pair(d).wait_recv()
            sbuf[d] = x_ref[place(core, ahead(d))] + pbuf[d]
            scatter(d).start()

        each(1, send_sum)
        pair(0).wait_recv()

        def add(d, acc):
            scatter(d).wait_recv()
            return acc + rbuf[d]

        o_ref[place(core, chip)] = lax.fori_loop(1, n, add, x_ref[place(core, chip)] + pbuf[0])
        each(1, lambda d: gather(d).start())
        forward(0).start()

        def pass_on(d):
            gathered(d).wait_recv()
            forward(d).start()

        each(1, pass_on)
        each(0, lambda d: forwarded(d).wait_recv())
        each(0, lambda d: pair(d).wait_send())
        each(1, lambda d: scatter(d).wait_send())
        each(1, lambda d: gather(d).wait_send())
        each(0, lambda d: forward(d).wait_send())

    def energy(local_ref, part, slots, sums):
        esend, erecv, csend, crecv = sums
        near = remote(local_ref, part, esend, erecv, partner)
        near.start()
        near.wait_recv()
        slots[chip] = local_ref[...] + part[...]

        def far(d, j):
            return remote(slots.at[j], slots.at[j], csend.at[d], crecv.at[d], device(ahead(d)))

        each(1, lambda d: far(d, chip).start())
        each(1, lambda d: far(d, behind(d)).wait_recv())
        near.wait_send()
        each(1, lambda d: far(d, chip).wait_send())
        return lax.fori_loop(1, n, lambda j, acc: acc + slots[j], slots[0])

    return greet, run, energy, remote, each


def piece_lanes(width, nd, nl):
    parts = nd * nl // GROUPS
    return -(-width // (parts * 128)) * 128


def exchange_scratch(lanes, nd, nl):
    n = nd // 2 * nl
    return [pltpu.VMEM((n, 8, lanes), jnp.float32)] * 3 + [pltpu.SemaphoreType.DMA((n,))] * 8


def first_kernel(nd, nl, x_ref, o_ref, pbuf, sbuf, rbuf, *sems):
    greet, run = exchange(nd, nl, x_ref, o_ref, pbuf, sbuf, rbuf, sems)[:2]
    greet()
    run()


def first_sum(x, nd, nl):
    lanes = x.shape[1] // (nd * nl // GROUPS)
    vmem = pl.BlockSpec(memory_space=pltpu.VMEM)
    return pl.pallas_call(
        functools.partial(first_kernel, nd, nl),
        out_shape=jax.ShapeDtypeStruct(x.shape, jnp.float32),
        in_specs=[vmem],
        out_specs=vmem,
        scratch_shapes=exchange_scratch(lanes, nd, nl),
        compiler_params=pltpu.CompilerParams(collective_id=2, has_side_effects=True, vmem_limit_bytes=40 << 20),
        name="first_sum",
    )(x)


def two_terms(x):
    high = x.astype(jnp.bfloat16)
    low = (x - high.astype(jnp.float32)).astype(jnp.bfloat16)
    return jnp.concatenate([high, low], axis=0)


def steps_kernel(
    nd, nl, scale, steps, c_ref, diag_ref, damp_ref, d0_ref, s0_ref, r0_ref, rho0_ref, w_ref, m_ref,
    d_ref, s_ref, rho_ref, energy_ref, wg_ref, mg_ref, r_ref, local_ref, part, slots, x_ref, o_ref,
    pbuf, sbuf, rbuf, *sems
):
    block, width = d_ref.shape
    greet, run, energy, remote, each = exchange(nd, nl, x_ref, o_ref, pbuf, sbuf, rbuf, sems[:8])
    wsend, wrecv, msend, mrecv = sems[8:12]
    dp = lax.axis_index("dp")
    label = lax.axis_index("label")
    own = m_ref.shape[1]
    share = -(-(nl - 1) // steps)

    def columns(at):
        return (slice(None), pl.ds(pl.multiple_of(at * own, 128), own))

    def beside(e, arriving):
        to = lax.rem(label + (nl - e if arriving else e), nl)
        at = to if arriving else label
        return (
            remote(w_ref, wg_ref.at[at], wsend.at[e], wrecv.at[e], (dp, to)),
            remote(m_ref, mg_ref.at[columns(at)], msend.at[e], mrecv.at[e], (dp, to)),
        )

    wg_ref[label] = w_ref[...]
    mg_ref[columns(label)] = m_ref[...]
    d_ref[...] = d0_ref[...]
    s_ref[...] = s0_ref[...]
    r_ref[...] = r0_ref[...]
    rho_ref[...] = rho0_ref[...]
    if x_ref.shape[1] > width:
        x_ref[:, width:] = jnp.zeros((block, x_ref.shape[1] - width), jnp.float32)
    tile = width // 3
    greet()

    def project():
        inner = lax.dot_general(
            two_terms(d_ref[...]), c_ref[...], (((1,), (1,)), ((), ())), preferred_element_type=jnp.float32
        )
        return inner[:block] + inner[block:]

    def update(g, carry):
        rows = pl.ds(pl.multiple_of(g * 32, 32), 32)
        direction = d_ref[rows, :]
        rho = rho_ref[rows, :]
        image = scale * o_ref[rows, :width] + damp_ref[...] * direction
        alpha = rho / jnp.sum(direction * image, axis=1, keepdims=True)
        s_ref[rows, :] = s_ref[rows, :] + alpha * direction
        resid = r_ref[rows, :] - alpha * image
        precond = resid / diag_ref[...]
        fresh = jnp.sum(resid * precond, axis=1, keepdims=True)
        r_ref[rows, :] = resid
        d_ref[rows, :] = precond + fresh / rho * direction
        rho_ref[rows, :] = fresh
        return carry

    def step(index, carry):
        first = 1 + index * share

        def send(e, carry):
            for copy in beside(e, False):
                copy.start()
            return carry

        lax.fori_loop(first, jnp.minimum(first + share, nl), send, 0)
        inner = two_terms(project())
        for begin in range(0, width, tile):
            cols = pl.ds(begin, tile)
            outer = jnp.dot(inner, c_ref[:, cols], preferred_element_type=jnp.float32)
            x_ref[:, cols] = outer[:block] + outer[block:]
        run()
        lax.fori_loop(0, block // 32, update, 0)
        return carry

    lax.fori_loop(0, steps, step, 0)
    inner = project()
    local_ref[...] = lax.dot_general(
        jnp.ones((8, inner.shape[1]), jnp.float32),
        inner * inner,
        (((1,), (1,)), ((), ())),
        precision=lax.Precision.HIGHEST,
        preferred_element_type=jnp.float32,
    )
    energy_ref[...] = energy(local_ref, part, slots, sems[12:])
    each(1, lambda e: [copy.wait_recv() for copy in beside(e, True)], nl)
    each(1, lambda e: [copy.wait_send() for copy in beside(e, False)], nl)


def middle_steps(calib, diag, damping, state, w, mask, scale, steps, nd, nl):
    block, width = state[0].shape
    lanes = piece_lanes(width + block, nd, nl)
    n = nd // 2 * nl
    padded = (block, lanes * (nd * nl // GROUPS))
    vmem = pl.BlockSpec(memory_space=pltpu.VMEM)
    whole = jax.ShapeDtypeStruct((block, width), jnp.float32)
    return pl.pallas_call(
        functools.partial(steps_kernel, nd, nl, scale, steps),
        out_shape=(
            whole,
            whole,
            jax.ShapeDtypeStruct((block, 1), jnp.float32),
            jax.ShapeDtypeStruct((8, block), jnp.float32),
            jax.ShapeDtypeStruct((nl,) + w.shape, w.dtype),
            jax.ShapeDtypeStruct((mask.shape[0], mask.shape[1] * nl), mask.dtype),
        ),
        in_specs=[vmem] * 9,
        out_specs=(vmem,) * 6,
        scratch_shapes=[pltpu.VMEM((block, width), jnp.float32)]
        + [pltpu.VMEM((8, block), jnp.float32)] * 2
        + [pltpu.VMEM((n, 8, block), jnp.float32)]
        + [pltpu.VMEM(padded, jnp.float32)] * 2
        + exchange_scratch(lanes, nd, nl)
        + [pltpu.SemaphoreType.DMA((nl,))] * 4
        + [pltpu.SemaphoreType.DMA] * 2
        + [pltpu.SemaphoreType.DMA((n,))] * 2,
        compiler_params=pltpu.CompilerParams(collective_id=0, has_side_effects=True, vmem_limit_bytes=52 << 20),
        name="middle_steps",
    )(calib, diag, damping, *state, w, mask)


def prune_kernel(w_ref, m_ref, l_ref, t_ref, kept_ref, err_ref, cross_ref):
    block = w_ref.shape[0]
    err_ref[...] = jnp.zeros_like(err_ref)
    cross_ref[...] = jnp.zeros_like(cross_ref)

    def earlier(factor, ref):
        return jnp.dot(factor, ref[...], precision=lax.Precision.HIGHEST, preferred_element_type=jnp.float32)

    for begin in range(0, block, sub_width):
        rows = pl.ds(begin, sub_width)
        window = w_ref[rows, :].astype(jnp.float32)
        target = t_ref[rows, :]
        chosen = m_ref[rows, :].astype(jnp.float32)
        factor = l_ref[rows, :]
        if begin:
            window = window - earlier(factor, err_ref)
            target = target - earlier(factor, cross_ref)
        for offset in range(sub_width):
            index = begin + offset
            one = slice(offset, offset + 1)
            column = factor[:, index : index + 1]
            inverse = 1.0 / factor[one, index : index + 1]
            error = chosen[one, :] * window[one, :] * inverse
            solved = target[one, :] * inverse
            err_ref[index : index + 1, :] = error
            cross_ref[index : index + 1, :] = solved
            window = window - column * error
            target = target - column * solved
        kept_ref[rows, :] = ((1.0 - chosen) * window).astype(kept_ref.dtype)


def prune_rows(weights, mask, lower, target):
    block, rows = weights.shape
    tile = min(rows, 2048)
    spec = pl.BlockSpec((block, tile), lambda i: (0, i))
    fixed = [pl.BlockSpec(x.shape, lambda i: (0, 0)) for x in (lower, target)]
    return pl.pallas_call(
        prune_kernel,
        grid=(rows // tile,),
        out_shape=(
            jax.ShapeDtypeStruct((block, rows), jnp.bfloat16),
            jax.ShapeDtypeStruct((block, rows), jnp.float32),
            jax.ShapeDtypeStruct(target.shape, jnp.float32),
        ),
        in_specs=[spec, spec] + fixed,
        out_specs=(spec, spec, fixed[1]),
        compiler_params=pltpu.CompilerParams(vmem_limit_bytes=32 << 20),
        name="prune_rows",
    )(weights, mask, lower, target)


def per_device(calib, block_weight, rest_weight, prune_mask):
    tokens = calib.shape[0]
    width = calib.shape[1]
    block = prune_mask.shape[1]
    nd, nl = lax.axis_size("dp"), lax.axis_size("label")
    total = tokens * nd * nl
    stat_rows = width // block
    padded = piece_lanes(width + block, nd, nl) * (nd * nl // GROUPS)
    local_sq = jnp.sum(jnp.square(calib.astype(jnp.float32)), axis=0)
    first = lax.dot_general(
        calib[:, :block], calib, (((0,), (0,)), ((), ())), preferred_element_type=jnp.float32
    )
    stats = jnp.pad(local_sq.reshape(stat_rows, block), ((0, block - stat_rows), (0, padded - width - block)))
    summed = first_sum(jnp.concatenate([first, stats], axis=1), nd, nl)
    colsq = summed[:stat_rows, width : width + block].reshape(1, width)
    damping = damp_fraction * 2.0 * jnp.sum(colsq) / (total * width)
    scale = 2.0 / total
    diag = scale * colsq + damping
    resid = jnp.eye(block, width, dtype=jnp.float32)
    precond = resid / diag
    direction = precond
    rho = jnp.sum(resid * precond, axis=1, keepdims=True)
    image = scale * (summed[:, :width] / diag[:, :block].T) + damping * direction
    alpha = rho / jnp.sum(direction * image, axis=1, keepdims=True)
    solution = alpha * direction
    resid = resid - alpha * image
    precond = resid / diag
    fresh = jnp.sum(resid * precond, axis=1, keepdims=True)
    direction = precond + fresh / rho * direction
    state = (direction, solution, resid, fresh)
    direction, solution, rho, norms, weights, mask = middle_steps(
        calib,
        diag,
        damping.reshape(1, 1),
        state,
        block_weight.T,
        prune_mask.T.astype(jnp.bfloat16),
        scale,
        ITERS - 2,
        nd,
        nl,
    )
    weights = weights.reshape(block, -1)
    energy = scale * norms[0] + damping * jnp.sum(direction * direction, axis=1)
    solution = solution + rho / energy[:, None] * direction
    top = 0.5 * (solution[:, :block] + solution[:, :block].T)
    lower = jnp.linalg.cholesky(top)
    own = prune_mask.shape[0]
    label = lax.axis_index("label")
    rest_cols = rest_weight.shape[1]
    owned = lax.dynamic_slice_in_dim(solution, block + label * rest_cols, rest_cols, 1)
    kept, errors, cross = prune_rows(weights, mask, lower, owned)
    pruned_block = lax.dynamic_slice_in_dim(kept, label * own, own, 1).T
    delta = lax.dot_general(
        errors,
        cross,
        (((0,), (0,)), ((), ())),
        precision=lax.Precision.HIGHEST,
        preferred_element_type=jnp.float32,
    )
    updated_rest = (rest_weight.astype(jnp.float32) - delta).astype(jnp.bfloat16)
    return (pruned_block, updated_rest)


def solution(mesh):
    return jax.shard_map(
        per_device,
        mesh=mesh,
        in_specs=(
            P(("dp", "label"), None),
            P("dp", "label"),
            P("dp", "label"),
            P(("dp", "label"), None),
        ),
        out_specs=(P(("dp", "label"), None), P("dp", "label")),
        check_vma=False,
    )
```

```python
import functools

import jax
import jax.numpy as jnp
from jax import lax
from jax.experimental import pallas as pl
from jax.experimental.pallas import tpu as pltpu
from jax.sharding import PartitionSpec as P

ITERS = 6
MESH = pl.DeviceIdType.MESH

damp_fraction = 0.01
sub_width = 16


GROUPS = 16


def exchange(nd, nl, x_ref, o_ref, pbuf, sbuf, rbuf, sems):
    psend, precv, ssend, srecv, gsend, grecv, fsend, frecv = sems
    dp = lax.axis_index("dp")
    label = lax.axis_index("label")
    core = lax.rem(dp, 2)
    chip = (dp // 2) * nl + label
    n = (nd // 2) * nl
    lanes = pbuf.shape[2]
    partner = (dp + 1 - 2 * core, label)

    def ahead(d):
        return lax.rem(chip + d, n)

    def behind(d):
        return lax.rem(chip + n - d, n)

    def device(j):
        return (2 * (j // nl) + core, lax.rem(j, nl))

    def place(half, j):
        q = half * n + j
        return (
            pl.ds(pl.multiple_of(lax.rem(q, GROUPS) * 8, 8), 8),
            pl.ds(pl.multiple_of((q // GROUPS) * lanes, 128), lanes),
        )

    def remote(src, dst, send, recv, to):
        return pltpu.make_async_remote_copy(
            src_ref=src, dst_ref=dst, send_sem=send, recv_sem=recv, device_id=to, device_id_type=MESH
        )

    def pair(d):
        return remote(x_ref.at[place(1 - core, ahead(d))], pbuf.at[d], psend.at[d], precv.at[d], partner)

    def scatter(d):
        return remote(sbuf.at[d], rbuf.at[d], ssend.at[d], srecv.at[d], device(ahead(d)))

    def gather(d):
        own = o_ref.at[place(core, chip)]
        return remote(own, own, gsend.at[d], grecv.at[d], device(ahead(d)))

    def gathered(d):
        ref = o_ref.at[place(core, behind(d))]
        return remote(ref, ref, gsend.at[d], grecv.at[d], device(behind(d)))

    def forward(d):
        ref = o_ref.at[place(core, behind(d))]
        return remote(ref, ref, fsend.at[d], frecv.at[d], partner)

    def forwarded(d):
        ref = o_ref.at[place(1 - core, behind(d))]
        return remote(ref, ref, fsend.at[d], frecv.at[d], partner)

    def each(low, body, high=n):
        def step(d, carry):
            body(d)
            return carry

        lax.fori_loop(low, high, step, 0)

    def greet():
        barrier = pltpu.get_barrier_semaphore()
        pl.semaphore_signal(barrier, inc=1, device_id=partner, device_id_type=MESH)
        each(1, lambda d: pl.semaphore_signal(barrier, inc=1, device_id=device(ahead(d)), device_id_type=MESH))
        pl.semaphore_wait(barrier, n)

    def run():
        each(1, lambda d: pair(d).start())
        pair(0).start()

        def send_sum(d):
            pair(d).wait_recv()
            sbuf[d] = x_ref[place(core, ahead(d))] + pbuf[d]
            scatter(d).start()

        each(1, send_sum)
        pair(0).wait_recv()

        def add(d, acc):
            scatter(d).wait_recv()
            return acc + rbuf[d]

        o_ref[place(core, chip)] = lax.fori_loop(1, n, add, x_ref[place(core, chip)] + pbuf[0])
        each(1, lambda d: gather(d).start())
        forward(0).start()

        def pass_on(d):
            gathered(d).wait_recv()
            forward(d).start()

        each(1, pass_on)
        each(0, lambda d: forwarded(d).wait_recv())
        each(0, lambda d: pair(d).wait_send())
        each(1, lambda d: scatter(d).wait_send())
        each(1, lambda d: gather(d).wait_send())
        each(0, lambda d: forward(d).wait_send())

    def energy(local_ref, part, slots, sums):
        esend, erecv, csend, crecv = sums
        near = remote(local_ref, part, esend, erecv, partner)
        near.start()
        near.wait_recv()
        slots[chip] = local_ref[...] + part[...]

        def far(d, j):
            return remote(slots.at[j], slots.at[j], csend.at[d], crecv.at[d], device(ahead(d)))

        each(1, lambda d: far(d, chip).start())
        each(1, lambda d: far(d, behind(d)).wait_recv())
        near.wait_send()
        each(1, lambda d: far(d, chip).wait_send())
        return lax.fori_loop(1, n, lambda j, acc: acc + slots[j], slots[0])

    return greet, run, energy, remote, each


def piece_lanes(width, nd, nl):
    parts = nd * nl // GROUPS
    return -(-width // (parts * 128)) * 128


def exchange_scratch(lanes, nd, nl):
    n = nd // 2 * nl
    return [pltpu.VMEM((n, 8, lanes), jnp.float32)] * 3 + [pltpu.SemaphoreType.DMA((n,))] * 8


def first_kernel(nd, nl, x_ref, o_ref, pbuf, sbuf, rbuf, *sems):
    greet, run = exchange(nd, nl, x_ref, o_ref, pbuf, sbuf, rbuf, sems)[:2]
    greet()
    run()


def first_sum(x, nd, nl):
    lanes = x.shape[1] // (nd * nl // GROUPS)
    vmem = pl.BlockSpec(memory_space=pltpu.VMEM)
    return pl.pallas_call(
        functools.partial(first_kernel, nd, nl),
        out_shape=jax.ShapeDtypeStruct(x.shape, jnp.float32),
        in_specs=[vmem],
        out_specs=vmem,
        scratch_shapes=exchange_scratch(lanes, nd, nl),
        compiler_params=pltpu.CompilerParams(collective_id=2, has_side_effects=True, vmem_limit_bytes=40 << 20),
        name="first_sum",
    )(x)


def two_terms(x):
    high = x.astype(jnp.bfloat16)
    low = (x - high.astype(jnp.float32)).astype(jnp.bfloat16)
    return jnp.concatenate([high, low], axis=0)


def steps_kernel(
    nd, nl, scale, steps, c_ref, diag_ref, damp_ref, d0_ref, s0_ref, r0_ref, rho0_ref, w_ref, m_ref,
    d_ref, s_ref, rho_ref, energy_ref, wg_ref, mg_ref, r_ref, local_ref, part, slots, x_ref, o_ref,
    pbuf, sbuf, rbuf, *sems
):
    block, width = d_ref.shape
    greet, run, energy, remote, each = exchange(nd, nl, x_ref, o_ref, pbuf, sbuf, rbuf, sems[:8])
    wsend, wrecv, msend, mrecv = sems[8:12]
    dp = lax.axis_index("dp")
    label = lax.axis_index("label")
    own = m_ref.shape[1]
    share = -(-(nl - 1) // steps)

    def columns(at):
        return (slice(None), pl.ds(pl.multiple_of(at * own, 128), own))

    def beside(e, arriving):
        to = lax.rem(label + (nl - e if arriving else e), nl)
        at = to if arriving else label
        return (
            remote(w_ref, wg_ref.at[at], wsend.at[e], wrecv.at[e], (dp, to)),
            remote(m_ref, mg_ref.at[columns(at)], msend.at[e], mrecv.at[e], (dp, to)),
        )

    wg_ref[label] = w_ref[...]
    mg_ref[columns(label)] = m_ref[...]
    d_ref[...] = d0_ref[...]
    s_ref[...] = s0_ref[...]
    r_ref[...] = r0_ref[...]
    rho_ref[...] = rho0_ref[...]
    if x_ref.shape[1] > width:
        x_ref[:, width:] = jnp.zeros((block, x_ref.shape[1] - width), jnp.float32)
    tile = width // 3
    greet()

    def project():
        inner = lax.dot_general(
            two_terms(d_ref[...]), c_ref[...], (((1,), (1,)), ((), ())), preferred_element_type=jnp.float32
        )
        return inner[:block] + inner[block:]

    def update(g, carry):
        rows = pl.ds(pl.multiple_of(g * 64, 64), 64)
        direction = d_ref[rows, :]
        rho = rho_ref[rows, :]
        image = scale * o_ref[rows, :width] + damp_ref[...] * direction
        alpha = rho / jnp.sum(direction * image, axis=1, keepdims=True)
        s_ref[rows, :] = s_ref[rows, :] + alpha * direction
        resid = r_ref[rows, :] - alpha * image
        precond = resid / diag_ref[...]
        fresh = jnp.sum(resid * precond, axis=1, keepdims=True)
        r_ref[rows, :] = resid
        d_ref[rows, :] = precond + fresh / rho * direction
        rho_ref[rows, :] = fresh
        return carry

    def step(index, carry):
        first = 1 + index * share

        def send(e, carry):
            for copy in beside(e, False):
                copy.start()
            return carry

        lax.fori_loop(first, jnp.minimum(first + share, nl), send, 0)
        inner = two_terms(project())
        for begin in range(0, width, tile):
            cols = pl.ds(begin, tile)
            outer = jnp.dot(inner, c_ref[:, cols], preferred_element_type=jnp.float32)
            x_ref[:, cols] = outer[:block] + outer[block:]
        run()
        lax.fori_loop(0, block // 64, update, 0)
        return carry

    lax.fori_loop(0, steps, step, 0)
    inner = project()
    local_ref[...] = lax.dot_general(
        jnp.ones((8, inner.shape[1]), jnp.float32),
        inner * inner,
        (((1,), (1,)), ((), ())),
        precision=lax.Precision.HIGHEST,
        preferred_element_type=jnp.float32,
    )
    energy_ref[...] = energy(local_ref, part, slots, sems[12:])
    each(1, lambda e: [copy.wait_recv() for copy in beside(e, True)], nl)
    each(1, lambda e: [copy.wait_send() for copy in beside(e, False)], nl)


def middle_steps(calib, diag, damping, state, w, mask, scale, steps, nd, nl):
    block, width = state[0].shape
    lanes = piece_lanes(width + block, nd, nl)
    n = nd // 2 * nl
    padded = (block, lanes * (nd * nl // GROUPS))
    vmem = pl.BlockSpec(memory_space=pltpu.VMEM)
    whole = jax.ShapeDtypeStruct((block, width), jnp.float32)
    return pl.pallas_call(
        functools.partial(steps_kernel, nd, nl, scale, steps),
        out_shape=(
            whole,
            whole,
            jax.ShapeDtypeStruct((block, 1), jnp.float32),
            jax.ShapeDtypeStruct((8, block), jnp.float32),
            jax.ShapeDtypeStruct((nl,) + w.shape, w.dtype),
            jax.ShapeDtypeStruct((mask.shape[0], mask.shape[1] * nl), mask.dtype),
        ),
        in_specs=[vmem] * 9,
        out_specs=(vmem,) * 6,
        scratch_shapes=[pltpu.VMEM((block, width), jnp.float32)]
        + [pltpu.VMEM((8, block), jnp.float32)] * 2
        + [pltpu.VMEM((n, 8, block), jnp.float32)]
        + [pltpu.VMEM(padded, jnp.float32)] * 2
        + exchange_scratch(lanes, nd, nl)
        + [pltpu.SemaphoreType.DMA((nl,))] * 4
        + [pltpu.SemaphoreType.DMA] * 2
        + [pltpu.SemaphoreType.DMA((n,))] * 2,
        compiler_params=pltpu.CompilerParams(collective_id=0, has_side_effects=True, vmem_limit_bytes=52 << 20),
        name="middle_steps",
    )(calib, diag, damping, *state, w, mask)


def prune_kernel(w_ref, m_ref, l_ref, t_ref, kept_ref, err_ref, cross_ref):
    block = w_ref.shape[0]
    err_ref[...] = jnp.zeros_like(err_ref)
    cross_ref[...] = jnp.zeros_like(cross_ref)

    def earlier(factor, ref):
        return jnp.dot(factor, ref[...], precision=lax.Precision.HIGHEST, preferred_element_type=jnp.float32)

    for begin in range(0, block, sub_width):
        rows = pl.ds(begin, sub_width)
        window = w_ref[rows, :].astype(jnp.float32)
        target = t_ref[rows, :]
        chosen = m_ref[rows, :].astype(jnp.float32)
        factor = l_ref[rows, :]
        if begin:
            window = window - earlier(factor, err_ref)
            target = target - earlier(factor, cross_ref)
        for offset in range(sub_width):
            index = begin + offset
            one = slice(offset, offset + 1)
            column = factor[:, index : index + 1]
            inverse = 1.0 / factor[one, index : index + 1]
            error = chosen[one, :] * window[one, :] * inverse
            solved = target[one, :] * inverse
            err_ref[index : index + 1, :] = error
            cross_ref[index : index + 1, :] = solved
            window = window - column * error
            target = target - column * solved
        kept_ref[rows, :] = ((1.0 - chosen) * window).astype(kept_ref.dtype)


def prune_rows(weights, mask, lower, target):
    block, rows = weights.shape
    tile = min(rows, 2048)
    spec = pl.BlockSpec((block, tile), lambda i: (0, i))
    fixed = [pl.BlockSpec(x.shape, lambda i: (0, 0)) for x in (lower, target)]
    return pl.pallas_call(
        prune_kernel,
        grid=(rows // tile,),
        out_shape=(
            jax.ShapeDtypeStruct((block, rows), jnp.bfloat16),
            jax.ShapeDtypeStruct((block, rows), jnp.float32),
            jax.ShapeDtypeStruct(target.shape, jnp.float32),
        ),
        in_specs=[spec, spec] + fixed,
        out_specs=(spec, spec, fixed[1]),
        compiler_params=pltpu.CompilerParams(vmem_limit_bytes=32 << 20),
        name="prune_rows",
    )(weights, mask, lower, target)


def per_device(calib, block_weight, rest_weight, prune_mask):
    tokens = calib.shape[0]
    width = calib.shape[1]
    block = prune_mask.shape[1]
    nd, nl = lax.axis_size("dp"), lax.axis_size("label")
    total = tokens * nd * nl
    stat_rows = width // block
    padded = piece_lanes(width + block, nd, nl) * (nd * nl // GROUPS)
    local_sq = jnp.sum(jnp.square(calib.astype(jnp.float32)), axis=0)
    first = lax.dot_general(
        calib[:, :block], calib, (((0,), (0,)), ((), ())), preferred_element_type=jnp.float32
    )
    stats = jnp.pad(local_sq.reshape(stat_rows, block), ((0, block - stat_rows), (0, padded - width - block)))
    summed = first_sum(jnp.concatenate([first, stats], axis=1), nd, nl)
    colsq = summed[:stat_rows, width : width + block].reshape(1, width)
    damping = damp_fraction * 2.0 * jnp.sum(colsq) / (total * width)
    scale = 2.0 / total
    diag = scale * colsq + damping
    resid = jnp.eye(block, width, dtype=jnp.float32)
    precond = resid / diag
    direction = precond
    rho = jnp.sum(resid * precond, axis=1, keepdims=True)
    image = scale * (summed[:, :width] / diag[:, :block].T) + damping * direction
    alpha = rho / jnp.sum(direction * image, axis=1, keepdims=True)
    solution = alpha * direction
    resid = resid - alpha * image
    precond = resid / diag
    fresh = jnp.sum(resid * precond, axis=1, keepdims=True)
    direction = precond + fresh / rho * direction
    state = (direction, solution, resid, fresh)
    direction, solution, rho, norms, weights, mask = middle_steps(
        calib,
        diag,
        damping.reshape(1, 1),
        state,
        block_weight.T,
        prune_mask.T.astype(jnp.bfloat16),
        scale,
        ITERS - 2,
        nd,
        nl,
    )
    weights = weights.reshape(block, -1)
    energy = scale * norms[0] + damping * jnp.sum(direction * direction, axis=1)
    solution = solution + rho / energy[:, None] * direction
    top = 0.5 * (solution[:, :block] + solution[:, :block].T)
    lower = jnp.linalg.cholesky(top)
    own = prune_mask.shape[0]
    label = lax.axis_index("label")
    rest_cols = rest_weight.shape[1]
    owned = lax.dynamic_slice_in_dim(solution, block + label * rest_cols, rest_cols, 1)
    kept, errors, cross = prune_rows(weights, mask, lower, owned)
    pruned_block = lax.dynamic_slice_in_dim(kept, label * own, own, 1).T
    delta = lax.dot_general(
        errors,
        cross,
        (((0,), (0,)), ((), ())),
        precision=lax.Precision.HIGHEST,
        preferred_element_type=jnp.float32,
    )
    updated_rest = (rest_weight.astype(jnp.float32) - delta).astype(jnp.bfloat16)
    return (pruned_block, updated_rest)


def solution(mesh):
    return jax.shard_map(
        per_device,
        mesh=mesh,
        in_specs=(
            P(("dp", "label"), None),
            P("dp", "label"),
            P("dp", "label"),
            P(("dp", "label"), None),
        ),
        out_specs=(P(("dp", "label"), None), P("dp", "label")),
        check_vma=False,
    )
```
